128 devices in a mesh: client: 16 (over y_lo, x, core), unit: 8 (over z, y_hi).
Axes of the slice: x: 4, y: 4 (y_hi: 2, y_lo: 2; y = y_hi * 2 + y_lo), z: 4, core: 2. Of those that a mesh axis runs over, the one named last changes fastest.
Arguments:
- token_ids: int32 [256], replicated, may hold values from 0 to 65535
- embed_table: bfloat16 [65536, 4096], P(('client', 'unit')), may hold values from -6 to 6
- norm_gain: float32 [4096], replicated, may hold values from 0.5 to 1.5
- client_gate: bfloat16 [16, 4096, 7168], P('client', None, 'unit'), may hold values from -0.09375 to 0.09375
- client_up: bfloat16 [16, 4096, 7168], P('client', None, 'unit'), may hold values from -0.09375 to 0.09375
- ref_gate: bfloat16 [4096, 7168], P('client', 'unit'), may hold values from -0.09375 to 0.09375
- ref_up: bfloat16 [4096, 7168], P('client', 'unit'), may hold values from -0.09375 to 0.09375
Outputs:
- merged: float32 [7168, 256], P('unit')
- score: float32 [16, 7168], P('client', 'unit')
The draws below stay inside these ranges and needn't reach their ends.
All inputs are finite; a program needn't handle non-finite values.
Results may differ from the reference program's by a relative error of at most 0.014.
Values may be sent and summed in bfloat16 or wider, within the bound.
A program may use at most 128 MiB of HBM per device.

```python
import math
import jax
import jax.numpy as jnp
import numpy as np
from jax import lax

D = 4096
FF = 7168
VOCAB = 65536
TOKENS = 256
CLIENTS = 16


def plant(values, stream_key, smallest, largest):
    longest = values.shape.index(max(values.shape))
    spots = []
    for shift in (0, 1):
        where = [jax.random.randint(jax.random.fold_in(stream_key, axis), (), 0, length) for axis, length in enumerate(values.shape)]
        where[longest] = (where[longest] + shift) % values.shape[longest]
        spots.append(tuple(where))
    return values.at[spots[0]].set(smallest).at[spots[1]].set(largest)


def shard_levels(key, dims, pieces, least, top_value):
    def one(position, shards_of):
        draws = jax.random.uniform(jax.random.fold_in(jax.random.fold_in(key, 6), position), (shards_of,), jnp.float32, least / len(pieces), top_value / len(pieces))
        return jnp.repeat(jnp.exp(draws), dims[position] // shards_of).reshape((-1,) + (1,) * (len(dims) - position - 1))

    factor_of = one(*pieces[0])
    for cut in pieces[1:]:
        factor_of = factor_of * one(*cut)
    return factor_of


def rank_table(number_of, slope):
    loads = [(1 << 20) // math.isqrt(grade ** slope) + 1 for grade in range(1, number_of + 1)]
    scale = 1 + sum(loads) // (1 << 30)
    return np.cumsum(np.array([max(1, weight // scale) for weight in loads]))


def ranked(stream_key, shape, amount, slope):
    listing = rank_table(amount, slope)
    lot = jax.random.randint(jax.random.fold_in(stream_key, 1), shape, 0, int(listing[amount - 1]))
    rank = jnp.searchsorted(jnp.asarray(listing, jnp.int32), lot, side="right")
    return jax.random.permutation(jax.random.fold_in(stream_key, 2), amount)[rank].astype(jnp.int32)


def normal_values(key, extent, width, bound, split=(), kind=jnp.bfloat16):
    entries = jax.random.normal(key, extent, jnp.float32) * width
    if len(split) > 0:
        entries = shard_levels(key, extent, split, -0.22, 0.18) * entries
    return jnp.clip(entries, min=-bound, max=bound).astype(kind)


def setup_inputs(seed: int = 0) -> dict:
    arg_keys = jax.random.split(jax.random.key(seed), 8)
    token_ids = plant(ranked(arg_keys[0], (TOKENS,), VOCAB, 2), jax.random.fold_in(arg_keys[0], 3), 0, VOCAB - 1).astype(jnp.int32)
    embed_table = normal_values(arg_keys[1], (VOCAB, D), 1.0, 6.0, ((0, 128),))
    norm_gain = jnp.clip(1.0 + 0.1 * jax.random.normal(arg_keys[2], (D,), jnp.float32), 0.5, 1.5)
    client_gate = normal_values(arg_keys[3], (CLIENTS, D, FF), D ** -0.5, 0.09375, ((0, 16), (2, 8)))
    client_up = normal_values(arg_keys[4], (CLIENTS, D, FF), D ** -0.5, 0.09375, ((0, 16), (2, 8)))
    ref_gate = normal_values(arg_keys[5], (D, FF), D ** -0.5, 0.09375, ((0, 16), (1, 8)))
    ref_up = normal_values(arg_keys[6], (D, FF), D ** -0.5, 0.09375, ((0, 16), (1, 8)))
    return {"token_ids": token_ids, "embed_table": embed_table, "norm_gain": norm_gain, "client_gate": client_gate, "client_up": client_up, "ref_gate": ref_gate, "ref_up": ref_up}


sharpness = 40.0

def standardize(hidden):
    center = lax.optimization_barrier(jnp.mean(hidden, axis=0, keepdims=True))
    shifted = hidden - center
    spread = jnp.sqrt(lax.optimization_barrier(jnp.mean(shifted * shifted, axis=0, keepdims=True)) + 1e-06)
    return (shifted / spread).astype(jnp.bfloat16)

def activate(normed, gate_weight, up_weight):
    gate = jnp.dot(normed, gate_weight, preferred_element_type=jnp.float32)
    up = jnp.dot(normed, up_weight, preferred_element_type=jnp.float32)
    return standardize(jax.nn.silu(gate) * up)

def reference(token_ids, embed_table, norm_gain, client_gate, client_up, ref_gate, ref_up):
    rows = jnp.take(embed_table, token_ids, axis=0).astype(jnp.float32)
    scale = lax.rsqrt(lax.optimization_barrier(jnp.mean(rows * rows, axis=1, keepdims=True)) + 1e-05)
    normed = (rows * scale * norm_gain[None, :]).astype(jnp.bfloat16)
    ref_std = activate(normed, ref_gate, ref_up)

    def per_client(total, pair):
        gate_weight, up_weight = pair
        client_std = activate(normed, gate_weight, up_weight)
        correlation = jnp.dot(client_std.T, ref_std, preferred_element_type=jnp.float32) * (1.0 / TOKENS)
        weights = jnp.exp(sharpness * correlation)
        colsum = lax.optimization_barrier(jnp.sum(weights, axis=0))
        weighted = lax.optimization_barrier(jnp.sum(weights * correlation, axis=0))
        numerator = lax.dot_general(weights.astype(jnp.bfloat16), client_std, (((0,), (1,)), ((), ())), preferred_element_type=jnp.float32)
        matched = numerator / colsum[:, None]
        return (total + matched, weighted / colsum)
    start_total = jnp.zeros((FF, TOKENS), jnp.float32)
    total, score = lax.scan(per_client, start_total, (client_gate, client_up))
    return (total / CLIENTS, score)
```

```python
import jax
import jax.numpy as jnp
from jax import lax
from jax.experimental import pallas as pl
from jax.experimental.pallas import tpu as pltpu
from jax.sharding import PartitionSpec as P

sharpness = 40.0
block_cols = 2048
MESH = pl.DeviceIdType.MESH

TOK = 256
D = 4096
HALF = D // 2
PARTS = ((0, 640), (640, 640), (1280, 768))
ORDERS = ("xyz", "yzx", "zxy")


class Place:
    def __init__(self):
        client = lax.axis_index("client")
        unit = lax.axis_index("unit")
        self.core = client % 2
        self.x = (client // 2) % 4
        self.y = (unit % 2) * 2 + client // 8
        self.z = unit // 2

    def at(self, axis):
        return getattr(self, axis)

    def peer(self, axis, step):
        x, y, z, core = self.x, self.y, self.z, self.core
        if axis == "x":
            x = (x + step) % 4
        elif axis == "y":
            y = (y + step) % 4
        elif axis == "z":
            z = (z + step) % 4
        else:
            core = 1 - core
        return {"client": (y % 2) * 8 + x * 2 + core, "unit": z * 2 + y // 2}


def send(src, dst, ssem, rsem, peer):
    copy = pltpu.make_async_remote_copy(
        src_ref=src, dst_ref=dst, send_sem=ssem, recv_sem=rsem, device_id=peer, device_id_type=MESH
    )
    copy.start()
    return copy


def rows(start, size):
    return pl.ds(pl.multiple_of(start, size), size)


def embed_kernel(ids_ref, gain_ref, table_ref, out_ref, *scratch):
    tabs = scratch[0:6]
    accs = scratch[6:9]
    outs = scratch[9:12]
    cins = scratch[12:15]
    r1s = scratch[15:18]
    a1s = scratch[18:21]
    r2s = scratch[21:24]
    a2s = scratch[24:27]
    r3s = scratch[27:30]
    fulls = scratch[30:33]
    tsem, ssem, rsem = scratch[33:36]
    me = Place()
    other = 1 - me.core

    loads = []
    for k in range(6):
        p = k % 3
        off, width = PARTS[p]
        half = other if k < 3 else me.core
        col = pl.multiple_of(half * HALF + off, 128)
        load = pltpu.make_async_copy(table_ref.at[:, pl.ds(col, width)], tabs[k], tsem.at[k])
        load.start()
        loads.append(load)

    barrier = pltpu.get_barrier_semaphore()
    peers = [me.peer(axis, step) for axis in "xyz" for step in (1, 2, 3)] + [me.peer("core", 1)]
    for peer in peers:
        pl.semaphore_signal(barrier, inc=1, device_id=peer, device_id_type=MESH)

    start = (lax.axis_index("client") * 8 + lax.axis_index("unit")) * 512
    table_rows = start + lax.broadcasted_iota(jnp.int32, (TOK, 512), 1)
    pick = jnp.where(ids_ref[...] == table_rows, 1.0, 0.0).astype(jnp.bfloat16)
    for p in range(3):
        loads[p].wait()
        outs[p][...] = jnp.dot(pick, tabs[p][...], preferred_element_type=jnp.float32).astype(jnp.bfloat16)
        if p == 0:
            pl.semaphore_wait(barrier, len(peers))
        loads[p] = send(outs[p], cins[p], ssem.at[p, 0, 0], rsem.at[p, 0, 0], me.peer("core", 1))
    sent = loads[:3]
    for p in range(3):
        loads[3 + p].wait()
        accs[p][...] = jnp.dot(pick, tabs[3 + p][...], preferred_element_type=jnp.float32).astype(jnp.bfloat16)

    s1 = [[], [], []]
    for p in range(3):
        sent[p].wait()
        accs[p][...] = accs[p][...] + cins[p][...]
        axis = ORDERS[p][0]
        for d in (1, 2, 3):
            to = (me.at(axis) + d) % 4
            s1[p].append(
                send(accs[p].at[rows(to * 64, 64)], r1s[p].at[d - 1], ssem.at[p, 1, d - 1], rsem.at[p, 1, d - 1], me.peer(axis, d))
            )
    s2 = [[], [], []]
    for p in range(3):
        for copy in s1[p]:
            copy.wait()
        own = accs[p][rows(me.at(ORDERS[p][0]) * 64, 64), :]
        a1s[p][...] = (own + r1s[p][0]) + (r1s[p][1] + r1s[p][2])
        axis = ORDERS[p][1]
        for d in (1, 2, 3):
            to = (me.at(axis) + d) % 4
            s2[p].append(
                send(a1s[p].at[rows(to * 16, 16)], r2s[p].at[d - 1], ssem.at[p, 2, d - 1], rsem.at[p, 2, d - 1], me.peer(axis, d))
            )
    s3 = [[], [], []]
    for p in range(3):
        for copy in s2[p]:
            copy.wait()
        own = a1s[p][rows(me.at(ORDERS[p][1]) * 16, 16), :]
        a2s[p][...] = (own + r2s[p][0]) + (r2s[p][1] + r2s[p][2])
        axis = ORDERS[p][2]
        for d in (1, 2, 3):
            s3[p].append(
                send(a2s[p], r3s[p].at[d - 1], ssem.at[p, 3, d - 1], rsem.at[p, 3, d - 1], me.peer(axis, d))
            )
    s4 = [[], [], []]
    for p in range(3):
        for copy in s3[p]:
            copy.wait()
        base = me.at(ORDERS[p][0]) * 64 + me.at(ORDERS[p][1]) * 16
        piece = fulls[p].at[me.core, rows(base, 16)]
        piece[...] = (a2s[p][...] + r3s[p][0]) + (r3s[p][1] + r3s[p][2])
        axis = ORDERS[p][1]
        for d in (1, 2, 3):
            s4[p].append(send(piece, piece, ssem.at[p, 4, d - 1], rsem.at[p, 4, d - 1], me.peer(axis, d)))
    s5 = [[], [], []]
    s6 = [[], [], []]
    for p in range(3):
        for copy in s4[p]:
            copy.wait()
        axis = ORDERS[p][0]
        piece = fulls[p].at[me.core, rows(me.at(axis) * 64, 64)]
        for d in (1, 2, 3):
            s5[p].append(send(piece, piece, ssem.at[p, 5, d - 1], rsem.at[p, 5, d - 1], me.peer(axis, d)))
        s6[p].append(send(piece, piece, ssem.at[p, 6, 0], rsem.at[p, 6, 0], me.peer("core", 1)))
    for p in range(3):
        axis = ORDERS[p][0]
        for d in (1, 2, 3):
            s5[p][d - 1].wait()
            came = (me.at(axis) + 4 - d) % 4
            piece = fulls[p].at[me.core, rows(came * 64, 64)]
            s6[p].append(send(piece, piece, ssem.at[p, 6, d], rsem.at[p, 6, d], me.peer("core", 1)))
    for p in range(3):
        for copy in s6[p]:
            copy.wait()

    for t in range(0, TOK, 32):
        total = jnp.zeros((32, 1), jnp.float32)
        for p in range(3):
            for h in range(2):
                v = fulls[p][h, pl.ds(t, 32), :].astype(jnp.float32)
                total = total + jnp.sum(v * v, axis=1, keepdims=True)
        scale = lax.rsqrt(total * (1.0 / D) + 1e-05)
        for p, (off, width) in enumerate(PARTS):
            for h in range(2):
                v = fulls[p][h, pl.ds(t, 32), :].astype(jnp.float32)
                cols = pl.ds(h * HALF + off, width)
                out_ref[pl.ds(t, 32), cols] = (v * scale * gain_ref[:, cols]).astype(jnp.bfloat16)


def embed_norm(token_ids, norm_gain, embed_table):
    bf = jnp.bfloat16
    widths = [w for _, w in PARTS]
    shapes = [pltpu.VMEM((512, w), bf) for w in widths * 2]
    shapes += [pltpu.VMEM((TOK, w), bf) for w in widths * 3]
    shapes += [pltpu.VMEM((3, 64, w), bf) for w in widths]
    shapes += [pltpu.VMEM((64, w), bf) for w in widths]
    shapes += [pltpu.VMEM((3, 16, w), bf) for w in widths]
    shapes += [pltpu.VMEM((16, w), bf) for w in widths]
    shapes += [pltpu.VMEM((3, 16, w), bf) for w in widths]
    shapes += [pltpu.VMEM((2, TOK, w), bf) for w in widths]
    shapes += [
        pltpu.SemaphoreType.DMA((6,)),
        pltpu.SemaphoreType.DMA((3, 7, 4)),
        pltpu.SemaphoreType.DMA((3, 7, 4)),
    ]
    return pl.pallas_call(
        embed_kernel,
        out_shape=jax.ShapeDtypeStruct((TOK, D), bf),
        in_specs=[
            pl.BlockSpec(memory_space=pltpu.VMEM),
            pl.BlockSpec(memory_space=pltpu.VMEM),
            pl.BlockSpec(memory_space=pl.ANY),
        ],
        out_specs=pl.BlockSpec(memory_space=pltpu.VMEM),
        scratch_shapes=shapes,
        compiler_params=pltpu.CompilerParams(collective_id=0, has_side_effects=True, vmem_limit_bytes=40 << 20),
        name="embed_norm",
    )(token_ids[:, None], norm_gain[None, :], embed_table)


def split_up(shard, dim, count):
    before, after = (shard.shape[:dim], shard.shape[dim + 1 :])
    return jnp.moveaxis(shard.reshape(*before, count, -1, *after), dim, 0)


def summed_on_arrival(shard, axis, dim):
    count = lax.axis_size(axis)
    blocks = lax.all_to_all(split_up(shard, dim, count), axis, 0, 0, tiled=True)
    return jnp.sum(blocks, axis=0)


def sent_together(arrays, axis, dim, along):
    widths = [a.shape[along] for a in arrays]
    both = jnp.concatenate(arrays, axis=along)
    result = summed_on_arrival(both, axis, dim)
    return tuple(jnp.split(result, [sum(widths[:k]) for k in range(1, len(widths))], axis=along))


def laid_out(blocks, dim):
    dims = list(blocks.shape[1:])
    dims[dim] *= blocks.shape[0]
    return jnp.moveaxis(blocks, 0, dim).reshape(dims)


def copy_for_each(shard, axis):
    copies = jnp.broadcast_to(shard, (lax.axis_size(axis), *shard.shape))
    return lax.all_to_all(copies, axis, split_axis=0, concat_axis=0, tiled=True)


def gather_directly(shard, axis, dim):
    return laid_out(copy_for_each(shard, axis), dim)


def filled_up(lines, count):
    spare = -len(lines) % count
    return jnp.pad(lines, [(0, spare)] + [(0, 0)] * (lines.ndim - 1))


def sent_and_summed(shard, axis, dim):
    blocks = split_up(shard, dim, lax.axis_size(axis))
    arrived = lax.all_to_all(blocks, axis, split_axis=0, concat_axis=0, tiled=True)
    return arrived.astype(jnp.float32).sum(axis=0)


def nested_sum(shard, axes):
    lines = shard.reshape(-1, shard.shape[-1])
    padded = filled_up(lines, lax.axis_size(axes))
    whole = gather_directly(sent_and_summed(padded, axes, 0).astype(jnp.bfloat16), axes, 0)
    return lax.slice_in_dim(whole, 0, len(lines)).reshape(shard.shape).astype(jnp.float32)


def standardize(hidden):
    center = jnp.mean(hidden, axis=0, keepdims=True)
    shifted = hidden - center
    spread = jnp.sqrt(jnp.mean(shifted * shifted, axis=0, keepdims=True) + 1e-06)
    return (shifted / spread).astype(jnp.bfloat16)


def block_ranges(length):
    return [(offset, min(block_cols, length - offset)) for offset in range(0, length, block_cols)]


def body(token_ids, embed_table, norm_gain, client_gate, client_up, ref_gate, ref_up):
    normed = embed_norm(token_ids, norm_gain, embed_table)
    token_count = normed.shape[0]
    inverse_tokens = 1.0 / token_count
    gate_local = jnp.dot(normed, client_gate[0], preferred_element_type=jnp.float32)
    up_local = jnp.dot(normed, client_up[0], preferred_element_type=jnp.float32)
    client_std = standardize(jax.nn.silu(gate_local) * up_local)
    row_span = ref_gate.shape[0]
    normed_slice = lax.dynamic_slice_in_dim(
        normed, lax.axis_index("client") * row_span, row_span, 1
    )
    gate_part = jnp.dot(normed_slice, ref_gate, preferred_element_type=jnp.float32)
    up_part = jnp.dot(normed_slice, ref_up, preferred_element_type=jnp.float32)
    gate_share, up_share = sent_together((gate_part, up_part), "client", 1, 0)
    ref_piece = standardize(jax.nn.silu(gate_share) * up_share)
    ref_std = gather_directly(ref_piece, "client", 1)
    local_units = client_std.shape[1]
    segment = lax.all_gather(client_std, "unit", axis=1, tiled=True)
    numerator = jnp.zeros((local_units, token_count), jnp.float32)
    colsum = jnp.zeros((local_units,), jnp.float32)
    weighted = jnp.zeros((local_units,), jnp.float32)
    for offset, width in block_ranges(segment.shape[1]):
        columns = segment[:, offset : offset + width]
        correlation = (
            jnp.dot(columns.T, ref_std, preferred_element_type=jnp.float32) * inverse_tokens
        )
        weights = jnp.exp(sharpness * correlation)
        numerator = numerator + lax.dot_general(
            weights.astype(jnp.bfloat16),
            columns,
            (((0,), (1,)), ((), ())),
            preferred_element_type=jnp.float32,
        )
        colsum = colsum + jnp.sum(weights, axis=0)
        weighted = weighted + jnp.sum(weights * correlation, axis=0)
    numerator, colsum, weighted = (numerator, colsum, weighted)
    matched = numerator / colsum[:, None]
    score = (weighted / colsum)[None, :]
    merged = nested_sum(matched.astype(jnp.bfloat16), "client") / lax.axis_size("client")
    return (merged, score)


def solution(mesh):
    in_specs = (
        P(),
        P(("client", "unit"), None),
        P(),
        P("client", None, "unit"),
        P("client", None, "unit"),
        P("client", "unit"),
        P("client", "unit"),
    )
    out_specs = (P("unit", None), P("client", "unit"))
    return jax.shard_map(body, mesh=mesh, in_specs=in_specs, out_specs=out_specs, check_vma=False)
```

```python
import jax
import jax.numpy as jnp
from jax import lax
from jax.experimental import pallas as pl
from jax.experimental.pallas import tpu as pltpu
from jax.sharding import PartitionSpec as P

sharpness = 40.0
MESH = pl.DeviceIdType.MESH

TOK = 256
D = 4096
HALF = D // 2
PARTS = ((0, 640), (640, 640), (1280, 768))
ORDERS = ("xyz", "yzx", "zxy")


class Place:
    def __init__(self):
        client = lax.axis_index("client")
        unit = lax.axis_index("unit")
        self.core = client % 2
        self.x = (client // 2) % 4
        self.y = (unit % 2) * 2 + client // 8
        self.z = unit // 2

    def at(self, axis):
        return getattr(self, axis)

    def peer(self, axis, step):
        x, y, z, core = self.x, self.y, self.z, self.core
        if axis == "x":
            x = (x + step) % 4
        elif axis == "y":
            y = (y + step) % 4
        elif axis == "z":
            z = (z + step) % 4
        else:
            core = 1 - core
        return {"client": (y % 2) * 8 + x * 2 + core, "unit": z * 2 + y // 2}


    def plane_peer(self, dx, flip, hflip):
        x = (self.x + dx) % 4
        low = (self.y % 2 + flip) % 2
        high = (self.y // 2 + hflip) % 2
        return {"client": low * 8 + x * 2 + self.core, "unit": self.z * 2 + high}

    def plane_piece(self, dx, flip):
        return ((self.x + dx) % 4) * 2 + (self.y % 2 + flip) % 2


def send(src, dst, ssem, rsem, peer):
    copy = pltpu.make_async_remote_copy(
        src_ref=src, dst_ref=dst, send_sem=ssem, recv_sem=rsem, device_id=peer, device_id_type=MESH
    )
    copy.start()
    return copy


def rows(start, size):
    return pl.ds(pl.multiple_of(start, size), size)


def embed_kernel(ids_ref, gain_ref, table_ref, out_ref, *scratch):
    tabs = scratch[0:6]
    accs = scratch[6:9]
    outs = scratch[9:12]
    cins = scratch[12:15]
    r1s = scratch[15:18]
    a1s = scratch[18:21]
    r2s = scratch[21:24]
    a2s = scratch[24:27]
    r3s = scratch[27:30]
    fulls = scratch[30:33]
    tsem, ssem, rsem = scratch[33:36]
    me = Place()
    other = 1 - me.core

    loads = []
    for k in range(6):
        p = k % 3
        off, width = PARTS[p]
        half = other if k < 3 else me.core
        col = pl.multiple_of(half * HALF + off, 128)
        load = pltpu.make_async_copy(table_ref.at[:, pl.ds(col, width)], tabs[k], tsem.at[k])
        load.start()
        loads.append(load)

    barrier = pltpu.get_barrier_semaphore()
    peers = [me.peer(axis, step) for axis in "xyz" for step in (1, 2, 3)] + [me.peer("core", 1)]
    for peer in peers:
        pl.semaphore_signal(barrier, inc=1, device_id=peer, device_id_type=MESH)

    start = (lax.axis_index("client") * 8 + lax.axis_index("unit")) * 512
    table_rows = start + lax.broadcasted_iota(jnp.int32, (TOK, 512), 1)
    pick = jnp.where(ids_ref[...] == table_rows, 1.0, 0.0).astype(jnp.bfloat16)
    for p in range(3):
        loads[p].wait()
        outs[p][...] = jnp.dot(pick, tabs[p][...], preferred_element_type=jnp.float32).astype(jnp.bfloat16)
        if p == 0:
            pl.semaphore_wait(barrier, len(peers))
        loads[p] = send(outs[p], cins[p], ssem.at[p, 0, 0], rsem.at[p, 0, 0], me.peer("core", 1))
    sent = loads[:3]
    for p in range(3):
        loads[3 + p].wait()
        accs[p][...] = jnp.dot(pick, tabs[3 + p][...], preferred_element_type=jnp.float32).astype(jnp.bfloat16)

    s1 = [[], [], []]
    for p in range(3):
        sent[p].wait()
        accs[p][...] = accs[p][...] + cins[p][...]
        axis = ORDERS[p][0]
        for d in (1, 2, 3):
            to = (me.at(axis) + d) % 4
            s1[p].append(
                send(accs[p].at[rows(to * 64, 64)], r1s[p].at[d - 1], ssem.at[p, 1, d - 1], rsem.at[p, 1, d - 1], me.peer(axis, d))
            )
    s2 = [[], [], []]
    for p in range(3):
        for copy in s1[p]:
            copy.wait()
        own = accs[p][rows(me.at(ORDERS[p][0]) * 64, 64), :]
        a1s[p][...] = (own + r1s[p][0]) + (r1s[p][1] + r1s[p][2])
        axis = ORDERS[p][1]
        for d in (1, 2, 3):
            to = (me.at(axis) + d) % 4
            s2[p].append(
                send(a1s[p].at[rows(to * 16, 16)], r2s[p].at[d - 1], ssem.at[p, 2, d - 1], rsem.at[p, 2, d - 1], me.peer(axis, d))
            )
    s3 = [[], [], []]
    for p in range(3):
        for copy in s2[p]:
            copy.wait()
        own = a1s[p][rows(me.at(ORDERS[p][1]) * 16, 16), :]
        a2s[p][...] = (own + r2s[p][0]) + (r2s[p][1] + r2s[p][2])
        axis = ORDERS[p][2]
        for d in (1, 2, 3):
            s3[p].append(
                send(a2s[p], r3s[p].at[d - 1], ssem.at[p, 3, d - 1], rsem.at[p, 3, d - 1], me.peer(axis, d))
            )
    s4 = [[], [], []]
    for p in range(3):
        for copy in s3[p]:
            copy.wait()
        base = me.at(ORDERS[p][0]) * 64 + me.at(ORDERS[p][1]) * 16
        piece = fulls[p].at[me.core, rows(base, 16)]
        piece[...] = (a2s[p][...] + r3s[p][0]) + (r3s[p][1] + r3s[p][2])
        axis = ORDERS[p][1]
        for d in (1, 2, 3):
            s4[p].append(send(piece, piece, ssem.at[p, 4, d - 1], rsem.at[p, 4, d - 1], me.peer(axis, d)))
    s5 = [[], [], []]
    s6 = [[], [], []]
    for p in range(3):
        for copy in s4[p]:
            copy.wait()
        axis = ORDERS[p][0]
        piece = fulls[p].at[me.core, rows(me.at(axis) * 64, 64)]
        for d in (1, 2, 3):
            s5[p].append(send(piece, piece, ssem.at[p, 5, d - 1], rsem.at[p, 5, d - 1], me.peer(axis, d)))
        s6[p].append(send(piece, piece, ssem.at[p, 6, 0], rsem.at[p, 6, 0], me.peer("core", 1)))
    for p in range(3):
        axis = ORDERS[p][0]
        for d in (1, 2, 3):
            s5[p][d - 1].wait()
            came = (me.at(axis) + 4 - d) % 4
            piece = fulls[p].at[me.core, rows(came * 64, 64)]
            s6[p].append(send(piece, piece, ssem.at[p, 6, d], rsem.at[p, 6, d], me.peer("core", 1)))
    for p in range(3):
        for copy in s6[p]:
            copy.wait()

    for t in range(0, TOK, 32):
        total = jnp.zeros((32, 1), jnp.float32)
        for p in range(3):
            for h in range(2):
                v = fulls[p][h, pl.ds(t, 32), :].astype(jnp.float32)
                total = total + jnp.sum(v * v, axis=1, keepdims=True)
        scale = lax.rsqrt(total * (1.0 / D) + 1e-05)
        for p, (off, width) in enumerate(PARTS):
            for h in range(2):
                v = fulls[p][h, pl.ds(t, 32), :].astype(jnp.float32)
                cols = pl.ds(h * HALF + off, width)
                out_ref[pl.ds(t, 32), cols] = (v * scale * gain_ref[:, cols]).astype(jnp.bfloat16)


def embed_norm(token_ids, norm_gain, embed_table):
    bf = jnp.bfloat16
    widths = [w for _, w in PARTS]
    shapes = [pltpu.VMEM((512, w), bf) for w in widths * 2]
    shapes += [pltpu.VMEM((TOK, w), bf) for w in widths * 3]
    shapes += [pltpu.VMEM((3, 64, w), bf) for w in widths]
    shapes += [pltpu.VMEM((64, w), bf) for w in widths]
    shapes += [pltpu.VMEM((3, 16, w), bf) for w in widths]
    shapes += [pltpu.VMEM((16, w), bf) for w in widths]
    shapes += [pltpu.VMEM((3, 16, w), bf) for w in widths]
    shapes += [pltpu.VMEM((2, TOK, w), bf) for w in widths]
    shapes += [
        pltpu.SemaphoreType.DMA((6,)),
        pltpu.SemaphoreType.DMA((3, 7, 4)),
        pltpu.SemaphoreType.DMA((3, 7, 4)),
    ]
    return pl.pallas_call(
        embed_kernel,
        out_shape=jax.ShapeDtypeStruct((TOK, D), bf),
        in_specs=[
            pl.BlockSpec(memory_space=pltpu.VMEM),
            pl.BlockSpec(memory_space=pltpu.VMEM),
            pl.BlockSpec(memory_space=pl.ANY),
        ],
        out_specs=pl.BlockSpec(memory_space=pltpu.VMEM),
        scratch_shapes=shapes,
        compiler_params=pltpu.CompilerParams(collective_id=0, has_side_effects=True, vmem_limit_bytes=40 << 20),
        name="embed_norm",
    )(token_ids[:, None], norm_gain[None, :], embed_table)

FF_HERE = 896
PIECE = 112
JOINT = 2 * FF_HERE
JC = 224
SPANS = ((0, 256), (256, 256), (512, 256), (768, 128))
RING8 = [(dx, f) for dx in range(4) for f in range(2)][1:]
RING16 = [(dx, f, h) for h in range(2) for dx in range(4) for f in range(2)][1:]
EXP_SCALE = sharpness / TOK * 1.4426950408889634


def spread(h, axis):
    center = jnp.mean(h, axis=axis, keepdims=True)
    shifted = h - center
    width = jnp.sqrt(jnp.mean(shifted * shifted, axis=axis, keepdims=True) + 1e-06)
    return (shifted / width).astype(jnp.bfloat16)


def gated(g, u):
    return g / (1.0 + jnp.exp(-g)) * u


def align_kernel(
    x_ref, cg_ref, cu_ref, rg_ref, ru_ref, merged_ref, score_ref,
    w, rw, part, pin, tb, r2, swap, swin, refs, units, wts, num, cs, ws, col, colin,
    nout, nin, nsum, f2, fin, wsem, rwsem, csem, crsem, zs, zr, xs, xr,
):
    me = Place()
    core, other = me.core, 1 - me.core
    mate = me.peer("core", 1)

    refload = []
    for k, src in enumerate((rg_ref, ru_ref)):
        load = pltpu.make_async_copy(src, rw.at[k], rwsem.at[k])
        load.start()
        refload.append(load)
    wload = {}
    for q in range(3):
        for k, src in enumerate((cg_ref, cu_ref)):
            load = pltpu.make_async_copy(
                src.at[0, :, pl.ds(q * 256, 256)], w.at[q * 2 + k], wsem.at[q * 2 + k]
            )
            load.start()
            wload[q, k] = load
    for k, src in enumerate((cg_ref, cu_ref)):
        load = pltpu.make_async_copy(
            src.at[0, :, pl.ds(768, 128)], w.at[6, :, pl.ds(k * 128, 128)], wsem.at[6 + k]
        )
        load.start()
        wload[3, k] = load

    barrier = pltpu.get_barrier_semaphore()
    peers = [me.plane_peer(*r) for r in RING16] + [me.peer("z", 1), me.peer("z", 3), mate]
    for peer in peers:
        pl.semaphore_signal(barrier, inc=1, device_id=peer, device_id_type=MESH)

    span = pl.ds(pl.multiple_of(lax.axis_index("client") * 256, 256), 256)
    xpart = x_ref[:, span]
    for k in range(2):
        refload[k].wait()
        part[k] = jnp.dot(xpart, rw[k], preferred_element_type=jnp.float32).T
    pl.semaphore_wait(barrier, len(peers))
    c1 = send(part.at[other], pin, csem.at[0], crsem.at[0], mate)

    zcopies = []

    def client_block(q):
        start, width = SPANS[q]
        for k in range(2):
            wload[q, k].wait()
        if q < 3:
            g = jnp.dot(x_ref[...], w[q * 2], preferred_element_type=jnp.float32)
            u = jnp.dot(x_ref[...], w[q * 2 + 1], preferred_element_type=jnp.float32)
        else:
            both = jnp.dot(x_ref[...], w[6], preferred_element_type=jnp.float32)
            g, u = both[:, :128], both[:, 128:]
        cols = pl.ds(start, width)
        units[0, :, cols] = spread(gated(g, u), 0)
        mine = units.at[0, :, cols]
        zcopies.append((
            send(mine, units.at[1, :, cols], zs.at[0, q], zr.at[0, q], me.peer("z", 1)),
            send(mine, units.at[3, :, cols], zs.at[1, q], zr.at[1, q], me.peer("z", 3)),
        ))

    relays = []

    def relay(q):
        cols = pl.ds(*SPANS[q])
        if q in (0, 3):
            zcopies[q][0].wait_recv()
            relays.append(send(units.at[1, :, cols], units.at[2, :, cols], zs.at[2, q], zr.at[2, q], me.peer("z", 1)))
        else:
            zcopies[q][1].wait_recv()
            relays.append(send(units.at[3, :, cols], units.at[2, :, cols], zs.at[2, q], zr.at[2, q], me.peer("z", 3)))

    client_block(0)
    c1.wait()
    tb[...] = (part[core] + pin[...]).astype(jnp.bfloat16)
    c2 = []
    for n, (dx, f) in enumerate(RING8):
        rows_to = rows(me.plane_piece(dx, f) * PIECE, PIECE)
        c2.append(send(tb.at[rows_to], r2.at[n], xs.at[0, n], xr.at[0, n], me.plane_peer(dx, f, 0)))
    client_block(1)
    client_block(2)
    client_block(3)
    here = me.plane_piece(0, 0)
    total = tb[rows(here * PIECE, PIECE), :].astype(jnp.float32)
    for n in range(7):
        c2[n].wait()
        total = total + r2[n].astype(jnp.float32)
    swap[...] = total
    c3 = send(swap, swin, csem.at[1], crsem.at[1], mate)
    relay(0)
    c3.wait()
    mine = swap[...]
    theirs = swin[...]
    first = core == 0
    g = jnp.where(first, mine, theirs)
    u = jnp.where(first, theirs, mine)
    piece_rows = rows((me.y // 2) * FF_HERE + here * PIECE, PIECE)
    half = pl.ds(pl.multiple_of(core * 128, 128), 128)
    piece_std = spread(gated(g, u), 1)
    refs[piece_rows, half] = jnp.where(first, piece_std[:, :128], piece_std[:, 128:])
    c4 = []
    for n, (dx, f, h) in enumerate(RING16):
        piece = refs.at[piece_rows, half]
        c4.append(send(piece, piece, xs.at[1, n], xr.at[1, n], me.plane_peer(dx, f, h)))
    relay(1)
    for copy in c4:
        copy.wait()
    c5 = send(refs.at[:, half], refs.at[:, half], csem.at[2], crsem.at[2], mate)
    relay(2)
    c5.wait()

    def align(slot, first, block):
        @pl.loop(0, FF_HERE // JC)
        def _(t):
            js = rows(block * FF_HERE + t * JC, JC)
            r = refs[js, :]
            a = jnp.zeros((JC, 128), jnp.float32) if first else cs[js, :]
            b = jnp.zeros((JC, 128), jnp.float32) if first else ws[js, :]
            for start, width in SPANS:
                s = jnp.dot(r, units[slot, :, pl.ds(start, width)], preferred_element_type=jnp.float32)
                e = jnp.exp2(s * EXP_SCALE)
                wts[:, pl.ds(start, width)] = e.astype(jnp.bfloat16)
                es = e * s
                for o in range(0, width, 128):
                    a = a + e[:, o : o + 128]
                    b = b + es[:, o : o + 128]
            cs[js, :] = a
            ws[js, :] = b
            got = lax.dot_general(
                wts[...], units[slot], (((1,), (1,)), ((), ())), preferred_element_type=jnp.float32
            )
            num[js, :] = got if first else num[js, :] + got

    align(0, True, 0)
    align(0, True, 1)
    relay(3)
    for slot, way, forwarded in ((1, 0, (0, 3)), (3, 1, (1, 2))):
        for q in range(4):
            if q not in forwarded:
                zcopies[q][way].wait_recv()
        for block in range(2):
            align(slot, False, block)
    for copy in relays:
        copy.wait_recv()

    eye = lax.broadcasted_iota(jnp.int32, (128, 128), 0) == lax.broadcasted_iota(jnp.int32, (128, 128), 1)

    def to_row(v):
        return jnp.sum(jnp.where(eye, jnp.sum(v, axis=1, keepdims=True), 0.0), axis=0, keepdims=True)

    c6 = []
    for block in range(2):
        align(2, False, block)
        for q in range(7):
            js = pl.ds(block * FF_HERE + q * 128, 128)
            col[block, pl.ds(q, 1), :] = to_row(cs[js, :])
            col[block, pl.ds(q + 8, 1), :] = to_row(ws[js, :])
        c6.append(send(col.at[block], colin.at[block], csem.at[3 + block], crsem.at[3 + block], me.peer("y", 2)))

    c7 = []
    for block in range(2):
        c6[block].wait()
        for q in range(7):
            js = pl.ds(block * FF_HERE + q * 128, 128)
            inv = 1.0 / (col[block, pl.ds(q, 1), :] + colin[block, pl.ds(q, 1), :])
            inv = jnp.sum(jnp.where(eye, inv, 0.0), axis=1, keepdims=True)
            n = (num[js, :] * inv).astype(jnp.bfloat16)
            nout[0, js, :] = n[:, :128]
            nout[1, js, :] = n[:, 128:]
        bs = pl.ds(block * FF_HERE, FF_HERE)
        c7.append(send(nout.at[other, bs], nin.at[bs], csem.at[5 + block], crsem.at[5 + block], mate))

    mineblock = me.y // 2
    for q in range(7):
        below = col[mineblock, pl.ds(q, 1), :] + colin[mineblock, pl.ds(q, 1), :]
        above = col[mineblock, pl.ds(q + 8, 1), :] + colin[mineblock, pl.ds(q + 8, 1), :]
        score_ref[:, pl.ds(q * 128, 128)] = above / below * (1.0 / TOK)

    for block in range(2):
        c7[block].wait()
        bs = pl.ds(block * FF_HERE, FF_HERE)
        nsum[bs, :] = nout[core, bs, :] + nin[bs, :]
    c8 = []
    for n, (dx, f, h) in enumerate(RING16):
        to = ((me.y // 2 + h) % 2) * FF_HERE + me.plane_piece(dx, f) * PIECE
        c8.append(send(nsum.at[rows(to, PIECE)], f2.at[n], xs.at[2, n], xr.at[2, n], me.plane_peer(dx, f, h)))
    total = nsum[piece_rows, :].astype(jnp.float32)
    for n in range(15):
        c8[n].wait()
        total = total + f2[n].astype(jnp.float32)
    mine = fin.at[core, here]
    mine[...] = total.astype(jnp.bfloat16)
    c9 = []
    c10 = [send(mine, mine, csem.at[7], crsem.at[7], mate)]
    for n, (dx, f) in enumerate(RING8):
        c9.append(send(mine, mine, xs.at[3, n], xr.at[3, n], me.plane_peer(dx, f, 0)))
    for n, (dx, f) in enumerate(RING8):
        c9[n].wait()
        came = fin.at[core, me.plane_piece(4 - dx, f)]
        c10.append(send(came, came, csem.at[8 + n], crsem.at[8 + n], mate))
    for copy in c10:
        copy.wait()
    for s in range(8):
        for h in range(2):
            merged_ref[pl.ds(s * PIECE, PIECE), pl.ds(h * 128, 128)] = fin[h, s].astype(jnp.float32) * (1.0 / 16)

    for pair in zcopies:
        pair[0].wait_send()
        pair[1].wait_send()
    for copy in relays:
        copy.wait_send()


def aligned(normed, client_gate, client_up, ref_gate, ref_up):
    bf, f32 = jnp.bfloat16, jnp.float32
    dma = pltpu.SemaphoreType.DMA
    shapes = [
        pltpu.VMEM((7, D, 256), bf),
        pltpu.VMEM((2, 256, FF_HERE), bf),
        pltpu.VMEM((2, FF_HERE, TOK), f32),
        pltpu.VMEM((FF_HERE, TOK), f32),
        pltpu.VMEM((FF_HERE, TOK), bf),
        pltpu.VMEM((7, PIECE, TOK), bf),
        pltpu.VMEM((PIECE, TOK), f32),
        pltpu.VMEM((PIECE, TOK), f32),
        pltpu.VMEM((JOINT, TOK), bf),
        pltpu.VMEM((4, TOK, FF_HERE), bf),
        pltpu.VMEM((JC, FF_HERE), bf),
        pltpu.VMEM((JOINT, TOK), f32),
        pltpu.VMEM((JOINT, 128), f32),
        pltpu.VMEM((JOINT, 128), f32),
        pltpu.VMEM((2, 16, 128), f32),
        pltpu.VMEM((2, 16, 128), f32),
        pltpu.VMEM((2, JOINT, 128), bf),
        pltpu.VMEM((JOINT, 128), bf),
        pltpu.VMEM((JOINT, 128), bf),
        pltpu.VMEM((15, PIECE, 128), bf),
        pltpu.VMEM((2, 8, PIECE, 128), bf),
        dma((8,)), dma((2,)), dma((15,)), dma((15,)),
        dma((3, 4)), dma((3, 4)), dma((4, 15)), dma((4, 15)),
    ]
    vmem = pl.BlockSpec(memory_space=pltpu.VMEM)
    hbm = pl.BlockSpec(memory_space=pl.ANY)
    return pl.pallas_call(
        align_kernel,
        out_shape=(
            jax.ShapeDtypeStruct((FF_HERE, TOK), f32),
            jax.ShapeDtypeStruct((1, FF_HERE), f32),
        ),
        in_specs=[vmem, hbm, hbm, hbm, hbm],
        out_specs=(vmem, vmem),
        scratch_shapes=shapes,
        compiler_params=pltpu.CompilerParams(collective_id=1, has_side_effects=True, vmem_limit_bytes=56 << 20),
        name="align",
    )(normed, client_gate, client_up, ref_gate, ref_up)


def body(token_ids, embed_table, norm_gain, client_gate, client_up, ref_gate, ref_up):
    normed = embed_norm(token_ids, norm_gain, embed_table)
    return aligned(normed, client_gate, client_up, ref_gate, ref_up)


def solution(mesh):
    in_specs = (
        P(),
        P(("client", "unit"), None),
        P(),
        P("client", None, "unit"),
        P("client", None, "unit"),
        P("client", "unit"),
        P("client", "unit"),
    )
    out_specs = (P("unit", None), P("client", "unit"))
    return jax.shard_map(body, mesh=mesh, in_specs=in_specs, out_specs=out_specs, check_vma=False)
```

```python
import jax
import jax.numpy as jnp
from jax import lax
from jax.experimental import pallas as pl
from jax.experimental.pallas import tpu as pltpu
from jax.sharding import PartitionSpec as P

sharpness = 40.0
MESH = pl.DeviceIdType.MESH

TOK = 256
D = 4096
HALF = D // 2
PARTS = ((0, 640), (640, 640), (1280, 768))
ORDERS = ("xyz", "yzx", "zxy")


class Place:
    def __init__(self):
        client = lax.axis_index("client")
        unit = lax.axis_index("unit")
        self.core = client % 2
        self.x = (client // 2) % 4
        self.y = (unit % 2) * 2 + client // 8
        self.z = unit // 2

    def at(self, axis):
        return getattr(self, axis)

    def peer(self, axis, step):
        x, y, z, core = self.x, self.y, self.z, self.core
        if axis == "x":
            x = (x + step) % 4
        elif axis == "y":
            y = (y + step) % 4
        elif axis == "z":
            z = (z + step) % 4
        else:
            core = 1 - core
        return {"client": (y % 2) * 8 + x * 2 + core, "unit": z * 2 + y // 2}


    def plane_peer(self, dx, flip, hflip, cflip=0):
        x = (self.x + dx) % 4
        low = (self.y % 2 + flip) % 2
        high = (self.y // 2 + hflip) % 2
        return {"client": low * 8 + x * 2 + (self.core + cflip) % 2, "unit": self.z * 2 + high}

    def plane_piece(self, dx, flip):
        return ((self.x + dx) % 4) * 2 + (self.y % 2 + flip) % 2


def send(src, dst, ssem, rsem, peer):
    copy = pltpu.make_async_remote_copy(
        src_ref=src, dst_ref=dst, send_sem=ssem, recv_sem=rsem, device_id=peer, device_id_type=MESH
    )
    copy.start()
    return copy


def rows(start, size):
    return pl.ds(pl.multiple_of(start, size), size)

FF_HERE = 896
PIECE = 112
JOINT = 2 * FF_HERE
JC = 224
SHARES = (4, 3, 4, 4)
SPANS = ((0, 256), (256, 256), (512, 256), (768, 128))
RING8 = [(dx, f) for dx in range(4) for f in range(2)][1:]
CROSS = [(dx, f, c) for dx in range(4) for f in range(2) for c in range(2)][1:]
RING16 = [(dx, f, h) for h in range(2) for dx in range(4) for f in range(2)][1:]
EXP_SCALE = sharpness / TOK * 1.4426950408889634


def spread(h, axis):
    center = jnp.mean(h, axis=axis, keepdims=True)
    shifted = h - center
    width = jnp.sqrt(jnp.mean(shifted * shifted, axis=axis, keepdims=True) + 1e-06)
    return (shifted / width).astype(jnp.bfloat16)


def gated(g, u):
    return g / (1.0 + jnp.exp(-g)) * u


def kernel(ids_ref, gain_ref, table_ref, cg_ref, cu_ref, rg_ref, ru_ref, merged_ref, score_ref, *scratch):
    e = Refs(scratch)
    me = Place()
    core, other = me.core, 1 - me.core
    mate = me.peer("core", 1)
    client = lax.axis_index("client")
    ssem, rsem = e.ssem, e.rsem

    loads = []
    for k in range(6):
        p = k % 3
        off, width = PARTS[p]
        half = other if k < 3 else core
        at = pl.multiple_of(half * HALF + off, 128)
        load = pltpu.make_async_copy(table_ref.at[:, pl.ds(at, width)], e.tabs[k], e.tsem.at[k])
        load.start()
        loads.append(load)
        if k == 2:
            refload = []
            for t, src in enumerate((rg_ref, ru_ref)):
                load = pltpu.make_async_copy(src, e.rw.at[t], e.rwsem.at[t])
                load.start()
                refload.append(load)

    barrier = pltpu.get_barrier_semaphore()
    peers = [me.plane_peer(*r) for r in RING16] + [me.peer("z", d) for d in (1, 2, 3)] + [mate]
    peers += [me.plane_peer(dx, f, 0, 1) for dx, f in RING8]
    for peer in peers:
        pl.semaphore_signal(barrier, inc=1, device_id=peer, device_id_type=MESH)

    eye = lax.broadcasted_iota(jnp.int32, (128, 128), 0) == lax.broadcasted_iota(jnp.int32, (128, 128), 1)
    start = (client * 8 + lax.axis_index("unit")) * 512
    table_rows = (start + lax.broadcasted_iota(jnp.int32, (1, 512), 1)).astype(jnp.float32)
    for t in range(2):
        wide = ids_ref[:, pl.ds(t * 128, 128)].astype(jnp.float32)
        tall = jnp.sum(jnp.where(eye, wide, 0.0), axis=1, keepdims=True)
        e.pick[pl.ds(t * 128, 128), :] = jnp.where(tall == table_rows, 1.0, 0.0).astype(jnp.bfloat16)

    def looked_up(k):
        loads[k].wait()
        return jnp.dot(e.pick[...], e.tabs[k][...], preferred_element_type=jnp.float32).astype(jnp.bfloat16)

    sent = []
    for p in range(3):
        e.outs[p][...] = looked_up(p)
    pl.semaphore_wait(barrier, len(peers))
    for p in range(3):
        sent.append(send(e.outs[p], e.cins[p], ssem.at[p, 0, 0], rsem.at[p, 0, 0], mate))
    for p in range(3):
        e.accs[p][...] = looked_up(3 + p)
    wload = {}
    for q in range(3):
        for k, src in enumerate((cg_ref, cu_ref)):
            load = pltpu.make_async_copy(
                src.at[0, :, pl.ds(q * 256, 256)], e.w.at[q * 2 + k], e.wsem.at[q * 2 + k]
            )
            load.start()
            wload[q, k] = load
    for k, src in enumerate((cg_ref, cu_ref)):
        load = pltpu.make_async_copy(
            src.at[0, :, pl.ds(768, 128)], e.w.at[6, :, pl.ds(k * 128, 128)], e.wsem.at[6 + k]
        )
        load.start()
        wload[3, k] = load

    here = me.plane_piece(0, 0)
    depth = pl.ds(pl.multiple_of(client * 256, 256), 256)
    for t in range(2):
        refload[t].wait()
        e.rt[t] = e.rw[t].T
    e.wr[:, depth] = e.rt[core, rows(here * PIECE, PIECE), :]
    shared = []

    def share(count):
        for _ in range(count):
            n = len(shared)
            dx, f, c = CROSS[n]
            src = e.rt.at[(core + c) % 2, rows(me.plane_piece(dx, f) * PIECE, PIECE)]
            shared.append(send(src, e.wr.at[:, depth], e.ws_.at[n], e.wr_.at[n], me.plane_peer(dx, f, 0, c)))

    s1 = [[], [], []]
    for p in range(3):
        sent[p].wait()
        e.accs[p][...] = e.accs[p][...] + e.cins[p][...]
        axis = ORDERS[p][0]
        for d in (1, 2, 3):
            to = (me.at(axis) + d) % 4
            s1[p].append(
                send(e.accs[p].at[rows(to * 64, 64)], e.r1s[p].at[d - 1], ssem.at[p, 1, d - 1], rsem.at[p, 1, d - 1], me.peer(axis, d))
            )
    share(SHARES[0])
    s2 = [[], [], []]
    for p in range(3):
        for copy in s1[p]:
            copy.wait()
        own = e.accs[p][rows(me.at(ORDERS[p][0]) * 64, 64), :]
        e.a1s[p][...] = (own + e.r1s[p][0]) + (e.r1s[p][1] + e.r1s[p][2])
        axis = ORDERS[p][1]
        for d in (1, 2, 3):
            to = (me.at(axis) + d) % 4
            s2[p].append(
                send(e.a1s[p].at[rows(to * 16, 16)], e.r2s[p].at[d - 1], ssem.at[p, 2, d - 1], rsem.at[p, 2, d - 1], me.peer(axis, d))
            )
    share(SHARES[1])
    s3 = [[], [], []]
    for p in range(3):
        for copy in s2[p]:
            copy.wait()
        own = e.a1s[p][rows(me.at(ORDERS[p][1]) * 16, 16), :]
        e.a2s[p][...] = (own + e.r2s[p][0]) + (e.r2s[p][1] + e.r2s[p][2])
        axis = ORDERS[p][2]
        for d in (1, 2, 3):
            s3[p].append(
                send(e.a2s[p], e.r3s[p].at[d - 1], ssem.at[p, 3, d - 1], rsem.at[p, 3, d - 1], me.peer(axis, d))
            )
    share(SHARES[2])
    s4 = [[], [], []]
    for p in range(3):
        for copy in s3[p]:
            copy.wait()
        base = me.at(ORDERS[p][0]) * 64 + me.at(ORDERS[p][1]) * 16
        piece = e.fulls[p].at[core, rows(base, 16)]
        piece[...] = (e.a2s[p][...] + e.r3s[p][0]) + (e.r3s[p][1] + e.r3s[p][2])
        axis = ORDERS[p][1]
        for d in (1, 2, 3):
            s4[p].append(send(piece, piece, ssem.at[p, 4, d - 1], rsem.at[p, 4, d - 1], me.peer(axis, d)))
    share(SHARES[3])
    s5 = [[], [], []]
    s6 = [[], [], []]
    for p in range(3):
        for copy in s4[p]:
            copy.wait()
        axis = ORDERS[p][0]
        piece = e.fulls[p].at[core, rows(me.at(axis) * 64, 64)]
        for d in (1, 2, 3):
            s5[p].append(send(piece, piece, ssem.at[p, 5, d - 1], rsem.at[p, 5, d - 1], me.peer(axis, d)))
        s6[p].append(send(piece, piece, ssem.at[p, 6, 0], rsem.at[p, 6, 0], mate))
    for p in range(3):
        axis = ORDERS[p][0]
        for d in (1, 2, 3):
            s5[p][d - 1].wait()
            came = (me.at(axis) + 4 - d) % 4
            piece = e.fulls[p].at[core, rows(came * 64, 64)]
            s6[p].append(send(piece, piece, ssem.at[p, 6, d], rsem.at[p, 6, d], mate))
    for p in range(3):
        for copy in s6[p]:
            copy.wait()
    for t in range(0, TOK, 32):
        total = jnp.zeros((32, 1), jnp.float32)
        for p in range(3):
            for h in range(2):
                v = e.fulls[p][h, pl.ds(t, 32), :].astype(jnp.float32)
                total = total + jnp.sum(v * v, axis=1, keepdims=True)
        scale = lax.rsqrt(total * (1.0 / D) + 1e-05)
        for p, (off, width) in enumerate(PARTS):
            for h in range(2):
                v = e.fulls[p][h, pl.ds(t, 32), :].astype(jnp.float32)
                cols = pl.ds(h * HALF + off, width)
                e.x[pl.ds(t, 32), cols] = (v * scale * gain_ref[:, cols]).astype(jnp.bfloat16)

    for copy in shared:
        copy.wait()
    e.swap[...] = lax.dot_general(e.wr[...], e.x[...], (((1,), (1,)), ((), ())), preferred_element_type=jnp.float32)
    c3 = send(e.swap, e.swin, e.csem.at[1], e.crsem.at[1], mate)

    zcopies = []

    def client_block(q):
        start, width = SPANS[q]
        for k in range(2):
            wload[q, k].wait()
        if q < 3:
            g = jnp.dot(e.x[...], e.w[q * 2], preferred_element_type=jnp.float32)
            u = jnp.dot(e.x[...], e.w[q * 2 + 1], preferred_element_type=jnp.float32)
        else:
            both = jnp.dot(e.x[...], e.w[6], preferred_element_type=jnp.float32)
            g, u = both[:, :128], both[:, 128:]
        cols = pl.ds(start, width)
        e.units[0, :, cols] = spread(gated(g, u), 0)
        mine = e.units.at[0, :, cols]
        zcopies.append((
            send(mine, e.units.at[1, :, cols], e.zs.at[0, q], e.zr.at[0, q], me.peer("z", 1)),
            send(mine, e.units.at[3, :, cols], e.zs.at[1, q], e.zr.at[1, q], me.peer("z", 3)),
        ))

    relays = []

    def relay(q):
        cols = pl.ds(*SPANS[q])
        if q in (0, 3):
            zcopies[q][0].wait_recv()
            relays.append(send(e.units.at[1, :, cols], e.units.at[2, :, cols], e.zs.at[2, q], e.zr.at[2, q], me.peer("z", 1)))
        else:
            zcopies[q][1].wait_recv()
            relays.append(send(e.units.at[3, :, cols], e.units.at[2, :, cols], e.zs.at[2, q], e.zr.at[2, q], me.peer("z", 3)))

    client_block(0)
    c3.wait()
    mine = e.swap[...]
    theirs = e.swin[...]
    lead = core == 0
    g = jnp.where(lead, mine, theirs)
    u = jnp.where(lead, theirs, mine)
    high = me.y // 2
    piece_rows = rows(high * FF_HERE + here * PIECE, PIECE)
    half = pl.ds(pl.multiple_of(core * 128, 128), 128)
    piece_std = spread(gated(g, u), 1)
    e.refs[piece_rows, half] = jnp.where(lead, piece_std[:, :128], piece_std[:, 128:])
    piece = e.refs.at[piece_rows, half]
    for n, (dx, f, h) in enumerate(RING16, 1):
        send(piece, piece, e.xs.at[1, n], e.xr.at[1, n], me.plane_peer(dx, f, h))

    client_block(1)
    client_block(2)
    client_block(3)
    relay(0)
    relay(1)

    def ref_arrived(block):
        hop = (block + high) % 2
        for dx in range(4):
            for f in range(2):
                n = hop * 8 + dx * 2 + f

                def arrive():
                    pltpu.make_async_remote_copy(
                        src_ref=piece, dst_ref=piece, send_sem=e.xs.at[1, n], recv_sem=e.xr.at[1, n],
                        device_id=me.plane_peer(dx, f, hop), device_id_type=MESH,
                    ).wait()

                if dx == 0 and f == 0:
                    pl.when(hop != 0)(arrive)
                else:
                    arrive()
        part = e.refs.at[pl.ds(block * FF_HERE, FF_HERE), half]
        return send(part, part, e.csem.at[2 + block], e.crsem.at[2 + block], mate)

    def align(slot, first, block):
        @pl.loop(0, FF_HERE // JC)
        def _(t):
            js = rows(block * FF_HERE + t * JC, JC)
            r = e.refs[js, :]
            a = jnp.zeros((JC, 128), jnp.float32) if first else e.cs[js, :]
            b = jnp.zeros((JC, 128), jnp.float32) if first else e.ws[js, :]
            for start, width in SPANS:
                s = jnp.dot(r, e.units[slot, :, pl.ds(start, width)], preferred_element_type=jnp.float32)
                v = jnp.exp2(s * EXP_SCALE)
                e.wts[:, pl.ds(start, width)] = v.astype(jnp.bfloat16)
                vs = v * s
                for o in range(0, width, 128):
                    a = a + v[:, o : o + 128]
                    b = b + vs[:, o : o + 128]
            e.cs[js, :] = a
            e.ws[js, :] = b
            got = lax.dot_general(
                e.wts[...], e.units[slot], (((1,), (1,)), ((), ())), preferred_element_type=jnp.float32
            )
            e.num[js, :] = got if first else e.num[js, :] + got

    def to_row(v):
        return jnp.sum(jnp.where(eye, jnp.sum(v, axis=1, keepdims=True), 0.0), axis=0, keepdims=True)

    def join_start(block):
        for q in range(7):
            js = pl.ds(block * FF_HERE + q * 128, 128)
            e.col[block, pl.ds(q, 1), :] = to_row(e.cs[js, :])
            e.col[block, pl.ds(q + 8, 1), :] = to_row(e.ws[js, :])
        return send(e.col.at[block], e.colin.at[block], e.csem.at[4 + block], e.crsem.at[4 + block], me.peer("y", 2))

    def normalize(block):
        for q in range(7):
            js = pl.ds(block * FF_HERE + q * 128, 128)
            inv = 1.0 / (e.col[block, pl.ds(q, 1), :] + e.colin[block, pl.ds(q, 1), :])
            inv = jnp.sum(jnp.where(eye, inv, 0.0), axis=1, keepdims=True)
            n = (e.num[js, :] * inv).astype(jnp.bfloat16)
            e.nout[0, js, :] = n[:, :128]
            e.nout[1, js, :] = n[:, 128:]
        bs = pl.ds(block * FF_HERE, FF_HERE)
        return send(e.nout.at[other, bs], e.nin.at[bs], e.csem.at[6 + block], e.crsem.at[6 + block], mate)

    def plane_copy(block, dx, f):
        hop = (block + high) % 2
        n = hop * 8 + dx * 2 + f
        src = e.nsum.at[rows(block * FF_HERE + me.plane_piece(dx, f) * PIECE, PIECE)]
        return pltpu.make_async_remote_copy(
            src_ref=src, dst_ref=e.f2.at[n], send_sem=e.xs.at[2, n], recv_sem=e.xr.at[2, n],
            device_id=me.plane_peer(dx, f, hop), device_id_type=MESH,
        ), hop

    def reduce_start(block):
        bs = pl.ds(block * FF_HERE, FF_HERE)
        e.nsum[bs, :] = e.nout[core, bs, :] + e.nin[bs, :]
        for dx in range(4):
            for f in range(2):
                copy, hop = plane_copy(block, dx, f)
                if dx == 0 and f == 0:
                    pl.when(hop != 0)(copy.start)
                else:
                    copy.start()

    c5 = ref_arrived(0)
    relay(2)
    c5.wait()
    align(0, True, 0)
    relay(3)
    c5 = ref_arrived(1)
    for slot, way, forwarded in ((1, 0, (0, 3)), (3, 1, (1, 2))):
        for q in range(4):
            if q not in forwarded:
                zcopies[q][way].wait_recv()
        align(slot, False, 0)
    for copy in relays:
        copy.wait_recv()
    align(2, False, 0)
    c6 = join_start(0)
    c5.wait()
    align(0, True, 1)
    align(1, False, 1)
    c6.wait()
    c7 = normalize(0)
    align(3, False, 1)
    c7.wait()
    reduce_start(0)
    align(2, False, 1)
    c6 = join_start(1)
    c6.wait()
    c7 = normalize(1)
    for q in range(7):
        below = e.col[high, pl.ds(q, 1), :] + e.colin[high, pl.ds(q, 1), :]
        above = e.col[high, pl.ds(q + 8, 1), :] + e.colin[high, pl.ds(q + 8, 1), :]
        score_ref[:, pl.ds(q * 128, 128)] = above / below * (1.0 / TOK)
    c7.wait()
    reduce_start(1)
    total = e.nsum[piece_rows, :].astype(jnp.float32)
    for block in range(2):
        for dx in range(4):
            for f in range(2):
                copy, hop = plane_copy(block, dx, f)
                if dx == 0 and f == 0:
                    pl.when(hop != 0)(copy.wait)
                else:
                    copy.wait()
    for n in range(1, 16):
        total = total + e.f2[n].astype(jnp.float32)
    mine = e.fin.at[core, here]
    mine[...] = total.astype(jnp.bfloat16)
    c9 = []
    c10 = [send(mine, mine, e.csem.at[8], e.crsem.at[8], mate)]
    for n, (dx, f) in enumerate(RING8):
        c9.append(send(mine, mine, e.xs.at[3, n], e.xr.at[3, n], me.plane_peer(dx, f, 0)))
    for n, (dx, f) in enumerate(RING8):
        c9[n].wait()
        came = e.fin.at[core, me.plane_piece(4 - dx, f)]
        c10.append(send(came, came, e.csem.at[9 + n], e.crsem.at[9 + n], mate))
    for copy in c10:
        copy.wait()
    for s in range(8):
        for h in range(2):
            merged_ref[pl.ds(s * PIECE, PIECE), pl.ds(h * 128, 128)] = e.fin[h, s].astype(jnp.float32) * (1.0 / 16)
    for pair in zcopies:
        pair[0].wait_send()
        pair[1].wait_send()
    for copy in relays:
        copy.wait_send()


def layout():
    bf, f32 = jnp.bfloat16, jnp.float32
    dma = pltpu.SemaphoreType.DMA
    vm = pltpu.VMEM
    widths = [w for _, w in PARTS]
    return {
        "tabs": [vm((512, w), bf) for w in widths * 2],
        "accs": [vm((TOK, w), bf) for w in widths],
        "outs": [vm((TOK, w), bf) for w in widths],
        "cins": [vm((TOK, w), bf) for w in widths],
        "r1s": [vm((3, 64, w), bf) for w in widths],
        "a1s": [vm((64, w), bf) for w in widths],
        "r2s": [vm((3, 16, w), bf) for w in widths],
        "a2s": [vm((16, w), bf) for w in widths],
        "r3s": [vm((3, 16, w), bf) for w in widths],
        "fulls": [vm((2, TOK, w), bf) for w in widths],
        "pick": vm((TOK, 512), bf),
        "x": vm((TOK, D), bf),
        "w": vm((7, D, 256), bf),
        "rw": vm((2, 256, FF_HERE), bf),
        "rt": vm((2, FF_HERE, 256), bf),
        "wr": vm((PIECE, D), bf),
        "swap": vm((PIECE, TOK), f32),
        "swin": vm((PIECE, TOK), f32),
        "refs": vm((JOINT, TOK), bf),
        "units": vm((4, TOK, FF_HERE), bf),
        "wts": vm((JC, FF_HERE), bf),
        "num": vm((JOINT, TOK), f32),
        "cs": vm((JOINT, 128), f32),
        "ws": vm((JOINT, 128), f32),
        "col": vm((2, 16, 128), f32),
        "colin": vm((2, 16, 128), f32),
        "nout": vm((2, JOINT, 128), bf),
        "nin": vm((JOINT, 128), bf),
        "nsum": vm((JOINT, 128), bf),
        "f2": vm((16, PIECE, 128), bf),
        "fin": vm((2, 8, PIECE, 128), bf),
        "tsem": dma((6,)),
        "ssem": dma((3, 7, 4)),
        "rsem": dma((3, 7, 4)),
        "wsem": dma((8,)),
        "rwsem": dma((2,)),
        "ws_": dma((15,)),
        "wr_": dma((15,)),
        "csem": dma((16,)),
        "crsem": dma((16,)),
        "zs": dma((3, 4)),
        "zr": dma((3, 4)),
        "xs": dma((4, 16)),
        "xr": dma((4, 16)),
    }


class Refs:
    def __init__(self, scratch):
        left = list(scratch)
        for name, shape in layout().items():
            if isinstance(shape, list):
                setattr(self, name, [left.pop(0) for _ in shape])
            else:
                setattr(self, name, left.pop(0))


def body(token_ids, embed_table, norm_gain, client_gate, client_up, ref_gate, ref_up):
    shapes = []
    for shape in layout().values():
        shapes += shape if isinstance(shape, list) else [shape]
    vmem = pl.BlockSpec(memory_space=pltpu.VMEM)
    hbm = pl.BlockSpec(memory_space=pl.ANY)
    return pl.pallas_call(
        kernel,
        out_shape=(
            jax.ShapeDtypeStruct((FF_HERE, TOK), jnp.float32),
            jax.ShapeDtypeStruct((1, FF_HERE), jnp.float32),
        ),
        in_specs=[vmem, vmem, hbm, hbm, hbm, hbm, hbm],
        out_specs=(vmem, vmem),
        scratch_shapes=shapes,
        compiler_params=pltpu.CompilerParams(collective_id=0, has_side_effects=True, vmem_limit_bytes=60 << 20),
        name="soft_alignment",
    )(token_ids[None, :], norm_gain[None, :], embed_table, client_gate, client_up, ref_gate, ref_up)


def solution(mesh):
    in_specs = (
        P(),
        P(("client", "unit"), None),
        P(),
        P("client", None, "unit"),
        P("client", None, "unit"),
        P("client", "unit"),
        P("client", "unit"),
    )
    out_specs = (P("unit", None), P("client", "unit"))
    return jax.shard_map(body, mesh=mesh, in_specs=in_specs, out_specs=out_specs, check_vma=False)
```

```python
import jax
import jax.numpy as jnp
from jax import lax
from jax.experimental import pallas as pl
from jax.experimental.pallas import tpu as pltpu
from jax.sharding import PartitionSpec as P

sharpness = 40.0
MESH = pl.DeviceIdType.MESH

TOK = 256
D = 4096
HALF = D // 2
PARTS = ((0, 384), (384, 384), (768, 384), (1152, 384), (1536, 256), (1792, 256))
ORDERS = ("xyz", "yzx", "zxy") * 2
NP = len(PARTS)


class Place:
    def __init__(self):
        client = lax.axis_index("client")
        unit = lax.axis_index("unit")
        self.core = client % 2
        self.x = (client // 2) % 4
        self.y = (unit % 2) * 2 + client // 8
        self.z = unit // 2

    def at(self, axis):
        return getattr(self, axis)

    def peer(self, axis, step):
        x, y, z, core = self.x, self.y, self.z, self.core
        if axis == "x":
            x = (x + step) % 4
        elif axis == "y":
            y = (y + step) % 4
        elif axis == "z":
            z = (z + step) % 4
        else:
            core = 1 - core
        return {"client": (y % 2) * 8 + x * 2 + core, "unit": z * 2 + y // 2}


    def plane_peer(self, dx, flip, hflip, cflip=0):
        x = (self.x + dx) % 4
        low = (self.y % 2 + flip) % 2
        high = (self.y // 2 + hflip) % 2
        return {"client": low * 8 + x * 2 + (self.core + cflip) % 2, "unit": self.z * 2 + high}

    def plane_piece(self, dx, flip):
        return ((self.x + dx) % 4) * 2 + (self.y % 2 + flip) % 2


def send(src, dst, ssem, rsem, peer):
    copy = pltpu.make_async_remote_copy(
        src_ref=src, dst_ref=dst, send_sem=ssem, recv_sem=rsem, device_id=peer, device_id_type=MESH
    )
    copy.start()
    return copy


def rows(start, size):
    return pl.ds(pl.multiple_of(start, size), size)

FF_HERE = 896
PIECE = 112
JOINT = 2 * FF_HERE
JC = 896
SHARES = (6, 0, 5, 4)
SPANS = ((0, 256), (256, 256), (512, 256), (768, 128))
RING8 = [(dx, f) for dx in range(4) for f in range(2)][1:]
CROSS = [(dx, f, c) for dx in range(4) for f in range(2) for c in range(2)][1:]
RING16 = [(dx, f, h) for h in range(2) for dx in range(4) for f in range(2)][1:]
EXP_SCALE = sharpness / TOK * 1.4426950408889634


def spread(h, axis):
    center = jnp.mean(h, axis=axis, keepdims=True)
    shifted = h - center
    width = jnp.sqrt(jnp.mean(shifted * shifted, axis=axis, keepdims=True) + 1e-06)
    return (shifted / width).astype(jnp.bfloat16)


def gated(g, u):
    return g / (1.0 + jnp.exp(-g)) * u


def kernel(ids_ref, gain_ref, table_ref, cg_ref, cu_ref, rg_ref, ru_ref, merged_ref, score_ref, *scratch):
    e = Refs(scratch)
    me = Place()
    core, other = me.core, 1 - me.core
    mate = me.peer("core", 1)
    client = lax.axis_index("client")
    ssem, rsem = e.ssem, e.rsem

    refload = []
    for t, src in enumerate((rg_ref, ru_ref)):
        load = pltpu.make_async_copy(src, e.rw.at[t], e.rwsem.at[t])
        load.start()
        refload.append(load)
    loads = []
    for k in range(2 * NP):
        off, width = PARTS[k % NP]
        half = other if k < NP else core
        at = pl.multiple_of(half * HALF + off, 128)
        load = pltpu.make_async_copy(table_ref.at[:, pl.ds(at, width)], e.tabs[k], e.tsem.at[k])
        load.start()
        loads.append(load)

    barrier = pltpu.get_barrier_semaphore()
    peers = [me.plane_peer(*r) for r in RING16] + [me.peer("z", d) for d in (1, 2, 3)] + [mate]
    peers += [me.plane_peer(dx, f, 0, 1) for dx, f in RING8]
    for peer in peers:
        pl.semaphore_signal(barrier, inc=1, device_id=peer, device_id_type=MESH)

    eye = lax.broadcasted_iota(jnp.int32, (128, 128), 0) == lax.broadcasted_iota(jnp.int32, (128, 128), 1)
    start = (client * 8 + lax.axis_index("unit")) * 512
    table_rows = (start + lax.broadcasted_iota(jnp.int32, (1, 512), 1)).astype(jnp.float32)
    for t in range(2):
        wide = ids_ref[:, pl.ds(t * 128, 128)].astype(jnp.float32)
        tall = jnp.sum(jnp.where(eye, wide, 0.0), axis=1, keepdims=True)
        e.pick[pl.ds(t * 128, 128), :] = jnp.where(tall == table_rows, 1.0, 0.0).astype(jnp.bfloat16)

    def looked_up(k):
        loads[k].wait()
        return jnp.dot(e.pick[...], e.tabs[k][...], preferred_element_type=jnp.float32).astype(jnp.bfloat16)

    here = me.plane_piece(0, 0)
    depth = pl.ds(pl.multiple_of(client * 256, 256), 256)
    for t in range(2):
        refload[t].wait()
        e.rt[t] = e.rw[t].T
    e.wr[:, depth] = e.rt[core, rows(here * PIECE, PIECE), :]
    shared = []

    def share(count):
        for _ in range(count):
            n = len(shared)
            dx, f, c = CROSS[n]
            src = e.rt.at[(core + c) % 2, rows(me.plane_piece(dx, f) * PIECE, PIECE)]
            shared.append(send(src, e.wr.at[:, depth], e.ws_.at[n], e.wr_.at[n], me.plane_peer(dx, f, 0, c)))

    pl.semaphore_wait(barrier, len(peers))
    share(SHARES[0])
    sent = []
    for p in range(NP):
        e.outs[p][...] = looked_up(p)
        sent.append(send(e.outs[p], e.cins[p], ssem.at[p, 0, 0], rsem.at[p, 0, 0], mate))
    for p in range(NP):
        e.accs[p][...] = looked_up(NP + p)
    wload = {}
    for q in range(3):
        for k, src in enumerate((cg_ref, cu_ref)):
            load = pltpu.make_async_copy(
                src.at[0, :, pl.ds(q * 256, 256)], e.w.at[q * 2 + k], e.wsem.at[q * 2 + k]
            )
            load.start()
            wload[q, k] = load
    for k, src in enumerate((cg_ref, cu_ref)):
        load = pltpu.make_async_copy(
            src.at[0, :, pl.ds(768, 128)], e.w.at[6, :, pl.ds(k * 128, 128)], e.wsem.at[6 + k]
        )
        load.start()
        wload[3, k] = load

    s1 = [[] for _ in range(NP)]
    for p in range(NP):
        sent[p].wait()
        e.accs[p][...] = e.accs[p][...] + e.cins[p][...]
        axis = ORDERS[p][0]
        for d in (1, 2, 3):
            to = (me.at(axis) + d) % 4
            s1[p].append(
                send(e.accs[p].at[rows(to * 64, 64)], e.r1s[p].at[d - 1], ssem.at[p, 1, d - 1], rsem.at[p, 1, d - 1], me.peer(axis, d))
            )
    s2 = [[] for _ in range(NP)]
    for p in range(NP):
        for copy in s1[p]:
            copy.wait()
        own = e.accs[p][rows(me.at(ORDERS[p][0]) * 64, 64), :]
        e.a1s[p][...] = (own + e.r1s[p][0]) + (e.r1s[p][1] + e.r1s[p][2])
        axis = ORDERS[p][1]
        for d in (1, 2, 3):
            to = (me.at(axis) + d) % 4
            s2[p].append(
                send(e.a1s[p].at[rows(to * 16, 16)], e.r2s[p].at[d - 1], ssem.at[p, 2, d - 1], rsem.at[p, 2, d - 1], me.peer(axis, d))
            )
    share(SHARES[1])
    s3 = [[] for _ in range(NP)]
    for p in range(NP):
        for copy in s2[p]:
            copy.wait()
        own = e.a1s[p][rows(me.at(ORDERS[p][1]) * 16, 16), :]
        e.a2s[p][...] = (own + e.r2s[p][0]) + (e.r2s[p][1] + e.r2s[p][2])
        axis = ORDERS[p][2]
        for d in (1, 2, 3):
            s3[p].append(
                send(e.a2s[p], e.r3s[p].at[d - 1], ssem.at[p, 3, d - 1], rsem.at[p, 3, d - 1], me.peer(axis, d))
            )
    share(SHARES[2])
    s4 = [[] for _ in range(NP)]
    for p in range(NP):
        for copy in s3[p]:
            copy.wait()
        base = me.at(ORDERS[p][0]) * 64 + me.at(ORDERS[p][1]) * 16
        piece = e.fulls[p].at[core, rows(base, 16)]
        piece[...] = (e.a2s[p][...] + e.r3s[p][0]) + (e.r3s[p][1] + e.r3s[p][2])
        axis = ORDERS[p][1]
        for d in (1, 2, 3):
            s4[p].append(send(piece, piece, ssem.at[p, 4, d - 1], rsem.at[p, 4, d - 1], me.peer(axis, d)))
    share(SHARES[3])
    s5 = [[] for _ in range(NP)]
    s6 = [[] for _ in range(NP)]
    for p in range(NP):
        for copy in s4[p]:
            copy.wait()
        axis = ORDERS[p][0]
        piece = e.fulls[p].at[core, rows(me.at(axis) * 64, 64)]
        for d in (1, 2, 3):
            s5[p].append(send(piece, piece, ssem.at[p, 5, d - 1], rsem.at[p, 5, d - 1], me.peer(axis, d)))
        s6[p].append(send(piece, piece, ssem.at[p, 6, 0], rsem.at[p, 6, 0], mate))
    for p in range(NP):
        axis = ORDERS[p][0]
        for d in (1, 2, 3):
            s5[p][d - 1].wait()
            came = (me.at(axis) + 4 - d) % 4
            piece = e.fulls[p].at[core, rows(came * 64, 64)]
            s6[p].append(send(piece, piece, ssem.at[p, 6, d], rsem.at[p, 6, d], mate))
    for p in range(NP):
        for copy in s6[p]:
            copy.wait()
    for t in range(0, TOK, 32):
        total = jnp.zeros((32, 1), jnp.float32)
        for p in range(NP):
            for h in range(2):
                v = e.fulls[p][h, pl.ds(t, 32), :].astype(jnp.float32)
                total = total + jnp.sum(v * v, axis=1, keepdims=True)
        scale = lax.rsqrt(total * (1.0 / D) + 1e-05)
        for p, (off, width) in enumerate(PARTS):
            for h in range(2):
                v = e.fulls[p][h, pl.ds(t, 32), :].astype(jnp.float32)
                cols = pl.ds(h * HALF + off, width)
                e.x[pl.ds(t, 32), cols] = (v * scale * gain_ref[:, cols]).astype(jnp.bfloat16)

    zcopies = []

    def client_block(q):
        start, width = SPANS[q]
        for k in range(2):
            wload[q, k].wait()
        if q < 3:
            g = jnp.dot(e.x[...], e.w[q * 2], preferred_element_type=jnp.float32)
            u = jnp.dot(e.x[...], e.w[q * 2 + 1], preferred_element_type=jnp.float32)
        else:
            both = jnp.dot(e.x[...], e.w[6], preferred_element_type=jnp.float32)
            g, u = both[:, :128], both[:, 128:]
        cols = pl.ds(start, width)
        e.units[0, :, cols] = spread(gated(g, u), 0)
        mine = e.units.at[0, :, cols]
        zcopies.append((
            send(mine, e.units.at[1, :, cols], e.zs.at[0, q], e.zr.at[0, q], me.peer("z", 1)),
            send(mine, e.units.at[3, :, cols], e.zs.at[1, q], e.zr.at[1, q], me.peer("z", 3)),
        ))

    relays = []

    def relay(q):
        cols = pl.ds(*SPANS[q])
        if q in (0, 3):
            zcopies[q][0].wait_recv()
            relays.append(send(e.units.at[1, :, cols], e.units.at[2, :, cols], e.zs.at[2, q], e.zr.at[2, q], me.peer("z", 1)))
        else:
            zcopies[q][1].wait_recv()
            relays.append(send(e.units.at[3, :, cols], e.units.at[2, :, cols], e.zs.at[2, q], e.zr.at[2, q], me.peer("z", 3)))

    client_block(0)
    for copy in shared:
        copy.wait()
    e.swap[...] = lax.dot_general(e.wr[...], e.x[...], (((1,), (1,)), ((), ())), preferred_element_type=jnp.float32)
    c3 = send(e.swap, e.swin, e.csem.at[1], e.crsem.at[1], mate)

    client_block(1)
    c3.wait()
    mine = e.swap[...]
    theirs = e.swin[...]
    lead = core == 0
    g = jnp.where(lead, mine, theirs)
    u = jnp.where(lead, theirs, mine)
    high = me.y // 2
    piece_rows = rows(high * FF_HERE + here * PIECE, PIECE)
    half = pl.ds(pl.multiple_of(core * 128, 128), 128)
    piece_std = spread(gated(g, u), 1)
    e.refs[piece_rows, half] = jnp.where(lead, piece_std[:, :128], piece_std[:, 128:])
    piece = e.refs.at[piece_rows, half]

    def hand_out():
        for n, (dx, f, h) in enumerate(RING16, 1):
            send(piece, piece, e.xs.at[1, n], e.xr.at[1, n], me.plane_peer(dx, f, h))

    pl.when(high == 0)(hand_out)
    client_block(2)
    client_block(3)
    pl.when(high == 1)(hand_out)
    relay(0)

    def ref_arrived(block):
        hop = (block + high) % 2
        for dx in range(4):
            for f in range(2):
                n = hop * 8 + dx * 2 + f

                def arrive():
                    pltpu.make_async_remote_copy(
                        src_ref=piece, dst_ref=piece, send_sem=e.xs.at[1, n], recv_sem=e.xr.at[1, n],
                        device_id=me.plane_peer(dx, f, hop), device_id_type=MESH,
                    ).wait()

                if dx == 0 and f == 0:
                    pl.when(hop != 0)(arrive)
                else:
                    arrive()
        part = e.refs.at[pl.ds(block * FF_HERE, FF_HERE), half]
        return send(part, part, e.csem.at[2 + block], e.crsem.at[2 + block], mate)

    def align(slot, first, block):
        @pl.loop(0, FF_HERE // JC)
        def _(t):
            js = rows(block * FF_HERE + t * JC, JC)
            r = e.refs[js, :]
            a = jnp.zeros((JC, 128), jnp.float32) if first else e.cs[js, :]
            b = jnp.zeros((JC, 128), jnp.float32) if first else e.ws[js, :]
            for start, width in SPANS:
                s = jnp.dot(r, e.units[slot, :, pl.ds(start, width)], preferred_element_type=jnp.float32)
                v = jnp.exp2(s * EXP_SCALE)
                e.wts[:, pl.ds(start, width)] = v.astype(jnp.bfloat16)
                vs = v * s
                for o in range(0, width, 128):
                    a = a + v[:, o : o + 128]
                    b = b + vs[:, o : o + 128]
            e.cs[js, :] = a
            e.ws[js, :] = b
            got = lax.dot_general(
                e.wts[...], e.units[slot], (((1,), (1,)), ((), ())), preferred_element_type=jnp.float32
            )
            e.num[js, :] = got if first else e.num[js, :] + got

    def to_row(v):
        return jnp.sum(jnp.where(eye, jnp.sum(v, axis=1, keepdims=True), 0.0), axis=0, keepdims=True)

    def join_start(block):
        for q in range(7):
            js = pl.ds(block * FF_HERE + q * 128, 128)
            e.col[block, pl.ds(q, 1), :] = to_row(e.cs[js, :])
            e.col[block, pl.ds(q + 8, 1), :] = to_row(e.ws[js, :])
        return send(e.col.at[block], e.colin.at[block], e.csem.at[4 + block], e.crsem.at[4 + block], me.peer("y", 2))

    def normalize(block):
        for q in range(7):
            js = pl.ds(block * FF_HERE + q * 128, 128)
            inv = 1.0 / (e.col[block, pl.ds(q, 1), :] + e.colin[block, pl.ds(q, 1), :])
            inv = jnp.sum(jnp.where(eye, inv, 0.0), axis=1, keepdims=True)
            n = (e.num[js, :] * inv).astype(jnp.bfloat16)
            e.nout[0, js, :] = n[:, :128]
            e.nout[1, js, :] = n[:, 128:]
        bs = pl.ds(block * FF_HERE, FF_HERE)
        return send(e.nout.at[other, bs], e.nin.at[bs], e.csem.at[6 + block], e.crsem.at[6 + block], mate)

    def plane_copy(block, dx, f):
        hop = (block + high) % 2
        n = hop * 8 + dx * 2 + f
        src = e.nsum.at[rows(block * FF_HERE + me.plane_piece(dx, f) * PIECE, PIECE)]
        return pltpu.make_async_remote_copy(
            src_ref=src, dst_ref=e.f2.at[n], send_sem=e.xs.at[2, n], recv_sem=e.xr.at[2, n],
            device_id=me.plane_peer(dx, f, hop), device_id_type=MESH,
        ), hop

    def reduce_start(block):
        bs = pl.ds(block * FF_HERE, FF_HERE)
        e.nsum[bs, :] = e.nout[core, bs, :] + e.nin[bs, :]
        for dx in range(4):
            for f in range(2):
                copy, hop = plane_copy(block, dx, f)
                if dx == 0 and f == 0:
                    pl.when(hop != 0)(copy.start)
                else:
                    copy.start()

    c5 = ref_arrived(0)
    relay(1)
    c5.wait()
    align(0, True, 0)
    relay(2)
    c5 = ref_arrived(1)
    relay(3)
    c5.wait()
    align(0, True, 1)
    for way, forwarded in ((0, (0, 3)), (1, (1, 2))):
        for q in range(4):
            if q not in forwarded:
                zcopies[q][way].wait_recv()
    align(1, False, 0)
    align(3, False, 0)
    align(1, False, 1)
    align(3, False, 1)
    for copy in relays:
        copy.wait_recv()
    align(2, False, 0)
    c6 = join_start(0)
    align(2, False, 1)
    c6.wait()
    c7 = normalize(0)
    c6 = join_start(1)
    c7.wait()
    reduce_start(0)
    c6.wait()
    c7 = normalize(1)
    for q in range(7):
        below = e.col[high, pl.ds(q, 1), :] + e.colin[high, pl.ds(q, 1), :]
        above = e.col[high, pl.ds(q + 8, 1), :] + e.colin[high, pl.ds(q + 8, 1), :]
        score_ref[:, pl.ds(q * 128, 128)] = above / below * (1.0 / TOK)
    c7.wait()
    reduce_start(1)
    total = e.nsum[piece_rows, :].astype(jnp.float32)
    for block in range(2):
        for dx in range(4):
            for f in range(2):
                copy, hop = plane_copy(block, dx, f)
                if dx == 0 and f == 0:
                    pl.when(hop != 0)(copy.wait)
                else:
                    copy.wait()
    for n in range(1, 16):
        total = total + e.f2[n].astype(jnp.float32)
    mine = e.fin.at[core, here]
    mine[...] = total.astype(jnp.bfloat16)
    c9 = []
    c10 = [send(mine, mine, e.csem.at[8], e.crsem.at[8], mate)]
    for n, (dx, f) in enumerate(RING8):
        c9.append(send(mine, mine, e.xs.at[3, n], e.xr.at[3, n], me.plane_peer(dx, f, 0)))
    for n, (dx, f) in enumerate(RING8):
        c9[n].wait()
        came = e.fin.at[core, me.plane_piece(4 - dx, f)]
        c10.append(send(came, came, e.csem.at[9 + n], e.crsem.at[9 + n], mate))
    for copy in c10:
        copy.wait()
    for s in range(8):
        for h in range(2):
            merged_ref[pl.ds(s * PIECE, PIECE), pl.ds(h * 128, 128)] = e.fin[h, s].astype(jnp.float32) * (1.0 / 16)
    for pair in zcopies:
        pair[0].wait_send()
        pair[1].wait_send()
    for copy in relays:
        copy.wait_send()


def layout():
    bf, f32 = jnp.bfloat16, jnp.float32
    dma = pltpu.SemaphoreType.DMA
    vm = pltpu.VMEM
    widths = [w for _, w in PARTS]
    return {
        "tabs": [vm((512, w), bf) for w in widths * 2],
        "accs": [vm((TOK, w), bf) for w in widths],
        "outs": [vm((TOK, w), bf) for w in widths],
        "cins": [vm((TOK, w), bf) for w in widths],
        "r1s": [vm((3, 64, w), bf) for w in widths],
        "a1s": [vm((64, w), bf) for w in widths],
        "r2s": [vm((3, 16, w), bf) for w in widths],
        "a2s": [vm((16, w), bf) for w in widths],
        "r3s": [vm((3, 16, w), bf) for w in widths],
        "fulls": [vm((2, TOK, w), bf) for w in widths],
        "pick": vm((TOK, 512), bf),
        "x": vm((TOK, D), bf),
        "w": vm((7, D, 256), bf),
        "rw": vm((2, 256, FF_HERE), bf),
        "rt": vm((2, FF_HERE, 256), bf),
        "wr": vm((PIECE, D), bf),
        "swap": vm((PIECE, TOK), f32),
        "swin": vm((PIECE, TOK), f32),
        "refs": vm((JOINT, TOK), bf),
        "units": vm((4, TOK, FF_HERE), bf),
        "wts": vm((JC, FF_HERE), bf),
        "num": vm((JOINT, TOK), f32),
        "cs": vm((JOINT, 128), f32),
        "ws": vm((JOINT, 128), f32),
        "col": vm((2, 16, 128), f32),
        "colin": vm((2, 16, 128), f32),
        "nout": vm((2, JOINT, 128), bf),
        "nin": vm((JOINT, 128), bf),
        "nsum": vm((JOINT, 128), bf),
        "f2": vm((16, PIECE, 128), bf),
        "fin": vm((2, 8, PIECE, 128), bf),
        "tsem": dma((2 * NP,)),
        "ssem": dma((NP, 7, 4)),
        "rsem": dma((NP, 7, 4)),
        "wsem": dma((8,)),
        "rwsem": dma((2,)),
        "ws_": dma((15,)),
        "wr_": dma((15,)),
        "csem": dma((16,)),
        "crsem": dma((16,)),
        "zs": dma((3, 4)),
        "zr": dma((3, 4)),
        "xs": dma((4, 16)),
        "xr": dma((4, 16)),
    }


class Refs:
    def __init__(self, scratch):
        left = list(scratch)
        for name, shape in layout().items():
            if isinstance(shape, list):
                setattr(self, name, [left.pop(0) for _ in shape])
            else:
                setattr(self, name, left.pop(0))


def body(token_ids, embed_table, norm_gain, client_gate, client_up, ref_gate, ref_up):
    shapes = []
    for shape in layout().values():
        shapes += shape if isinstance(shape, list) else [shape]
    vmem = pl.BlockSpec(memory_space=pltpu.VMEM)
    hbm = pl.BlockSpec(memory_space=pl.ANY)
    return pl.pallas_call(
        kernel,
        out_shape=(
            jax.ShapeDtypeStruct((FF_HERE, TOK), jnp.float32),
            jax.ShapeDtypeStruct((1, FF_HERE), jnp.float32),
        ),
        in_specs=[vmem, vmem, hbm, hbm, hbm, hbm, hbm],
        out_specs=(vmem, vmem),
        scratch_shapes=shapes,
        compiler_params=pltpu.CompilerParams(collective_id=0, has_side_effects=True, vmem_limit_bytes=60 << 20),
        name="soft_alignment",
    )(token_ids[None, :], norm_gain[None, :], embed_table, client_gate, client_up, ref_gate, ref_up)


def solution(mesh):
    in_specs = (
        P(),
        P(("client", "unit"), None),
        P(),
        P("client", None, "unit"),
        P("client", None, "unit"),
        P("client", "unit"),
        P("client", "unit"),
    )
    out_specs = (P("unit", None), P("client", "unit"))
    return jax.shard_map(body, mesh=mesh, in_specs=in_specs, out_specs=out_specs, check_vma=False)
```

```python
import jax
import jax.numpy as jnp
from jax import lax
from jax.experimental import pallas as pl
from jax.experimental.pallas import tpu as pltpu
from jax.sharding import PartitionSpec as P

sharpness = 40.0
MESH = pl.DeviceIdType.MESH

TOK = 256
D = 4096
HALF = D // 2
PARTS = ((0, 384), (384, 384), (768, 384), (1152, 384), (1536, 256), (1792, 256))
ORDERS = ("xyz", "yzx", "zxy") * 2
NP = len(PARTS)


class Place:
    def __init__(self):
        client = lax.axis_index("client")
        unit = lax.axis_index("unit")
        self.core = client % 2
        self.x = (client // 2) % 4
        self.y = (unit % 2) * 2 + client // 8
        self.z = unit // 2

    def at(self, axis):
        return getattr(self, axis)

    def peer(self, axis, step):
        x, y, z, core = self.x, self.y, self.z, self.core
        if axis == "x":
            x = (x + step) % 4
        elif axis == "y":
            y = (y + step) % 4
        elif axis == "z":
            z = (z + step) % 4
        else:
            core = 1 - core
        return {"client": (y % 2) * 8 + x * 2 + core, "unit": z * 2 + y // 2}


    def plane_peer(self, dx, flip, hflip, cflip=0):
        x = (self.x + dx) % 4
        low = (self.y % 2 + flip) % 2
        high = (self.y // 2 + hflip) % 2
        return {"client": low * 8 + x * 2 + (self.core + cflip) % 2, "unit": self.z * 2 + high}

    def plane_piece(self, dx, flip):
        return ((self.x + dx) % 4) * 2 + (self.y % 2 + flip) % 2


def send(src, dst, ssem, rsem, peer):
    copy = pltpu.make_async_remote_copy(
        src_ref=src, dst_ref=dst, send_sem=ssem, recv_sem=rsem, device_id=peer, device_id_type=MESH
    )
    copy.start()
    return copy


def drain(sem, ref):
    pltpu.make_async_copy(ref, ref, sem).wait()


def rows(start, size):
    return pl.ds(pl.multiple_of(start, size), size)

FF_HERE = 896
PIECE = 112
JOINT = 2 * FF_HERE
JC = 896
SHARES = (5, 3, 4, 3)
SPANS = ((0, 256), (256, 256), (512, 256), (768, 128))
RING8 = [(dx, f) for dx in range(4) for f in range(2)][1:]
CROSS = [(dx, f, c) for dx in range(4) for f in range(2) for c in range(2)][1:]
RING16 = [(dx, f, h) for h in range(2) for dx in range(4) for f in range(2)][1:]
EXP_SCALE = sharpness / TOK * 1.4426950408889634


def spread(h, axis):
    center = jnp.mean(h, axis=axis, keepdims=True)
    shifted = h - center
    width = jnp.sqrt(jnp.mean(shifted * shifted, axis=axis, keepdims=True) + 1e-06)
    return (shifted / width).astype(jnp.bfloat16)


def gated(g, u):
    return g / (1.0 + jnp.exp(-g)) * u


def kernel(ids_ref, gain_ref, table_ref, cg_ref, cu_ref, rg_ref, ru_ref, fin_ref, score_ref, *scratch):
    e = Refs(scratch)
    me = Place()
    core, other = me.core, 1 - me.core
    mate = me.peer("core", 1)
    client = lax.axis_index("client")
    ssem, rsem = e.ssem, e.rsem

    def table_load(k):
        half = other if k < 4 else core
        at = pl.multiple_of(half * HALF + k % 4 * 512, 512)
        load = pltpu.make_async_copy(table_ref.at[:, pl.ds(at, 512)], e.tabs.at[k], e.tsem.at[k])
        load.start()
        return load

    loads = [table_load(k) for k in range(8)]
    for t, src in enumerate((rg_ref, ru_ref)):
        pltpu.make_async_copy(src, e.rw.at[t], e.rwsem.at[0]).start()

    barrier = pltpu.get_barrier_semaphore()
    peers = [me.plane_peer(*r) for r in RING16] + [me.peer("z", d) for d in (1, 2, 3)] + [mate]
    peers += [me.plane_peer(dx, f, 0, 1) for dx, f in RING8]
    for peer in peers:
        pl.semaphore_signal(barrier, inc=1, device_id=peer, device_id_type=MESH)

    eye = lax.broadcasted_iota(jnp.int32, (128, 128), 0) == lax.broadcasted_iota(jnp.int32, (128, 128), 1)
    start = (client * 8 + lax.axis_index("unit")) * 512
    table_rows = (start + lax.broadcasted_iota(jnp.int32, (1, 512), 1)).astype(jnp.float32)
    for t in range(2):
        wide = ids_ref[:, pl.ds(t * 128, 128)].astype(jnp.float32)
        tall = jnp.sum(jnp.where(eye, wide, 0.0), axis=1, keepdims=True)
        e.pick[pl.ds(t * 128, 128), :] = jnp.where(tall == table_rows, 1.0, 0.0).astype(jnp.bfloat16)

    def looked_up(k):
        loads[k].wait()
        return jnp.dot(e.pick[...], e.tabs[k], preferred_element_type=jnp.float32).astype(jnp.bfloat16)

    chunks = [pl.ds(k * 512, 512) for k in range(4)]
    for k in range(4):
        e.outs[:, chunks[k]] = looked_up(k)
    pl.semaphore_wait(barrier, len(peers))
    sent = []
    for k in range(4):
        sent.append(send(e.outs.at[:, chunks[k]], e.cins.at[:, chunks[k]], e.csem.at[0], e.crsem.at[k], mate))
    for k in range(4):
        e.accs[:, chunks[k]] = looked_up(4 + k)
    wload = {}
    for q in range(3):
        for k, src in enumerate((cg_ref, cu_ref)):
            load = pltpu.make_async_copy(
                src.at[0, :, pl.ds(q * 256, 256)], e.w.at[q * 2 + k], e.wsem.at[q * 2 + k]
            )
            load.start()
            wload[q, k] = load
    for k, src in enumerate((cg_ref, cu_ref)):
        load = pltpu.make_async_copy(
            src.at[0, :, pl.ds(768, 128)], e.w.at[6, :, pl.ds(k * 128, 128)], e.wsem.at[6 + k]
        )
        load.start()
        wload[3, k] = load

    for k in range(4):
        sent[k].wait_recv()
        e.accs[:, chunks[k]] = e.accs[:, chunks[k]] + e.cins[:, chunks[k]]
    for p in range(NP):
        axis = ORDERS[p][0]
        for d in (1, 2, 3):
            to = (me.at(axis) + d) % 4
            src = e.accs.at[rows(to * 64, 64), pl.ds(*PARTS[p])]
            send(src, e.r1s[p].at[d - 1], ssem.at[p], rsem.at[p, 0], me.peer(axis, d))

    here = me.plane_piece(0, 0)
    depth = pl.ds(pl.multiple_of(client * 256, 256), 256)
    drain(e.rwsem.at[0], e.rw)
    for t in range(2):
        e.rt[t] = e.rw[t].T
    e.wr[:, depth] = e.rt[core, rows(here * PIECE, PIECE), :]
    shared = []

    def share(count):
        for _ in range(count):
            n = len(shared)
            dx, f, c = CROSS[n]
            src = e.rt.at[(core + c) % 2, rows(me.plane_piece(dx, f) * PIECE, PIECE)]
            shared.append(send(src, e.wr.at[:, depth], e.wshare.at[0], e.wshare.at[1], me.plane_peer(dx, f, 0, c)))

    share(SHARES[0])
    for p in range(NP):
        drain(rsem.at[p, 0], e.r1s[p])
        drain(ssem.at[p], e.r1s[p])
        own = e.accs[rows(me.at(ORDERS[p][0]) * 64, 64), pl.ds(*PARTS[p])]
        e.a1s[p][...] = (own + e.r1s[p][0]) + (e.r1s[p][1] + e.r1s[p][2])
        axis = ORDERS[p][1]
        for d in (1, 2, 3):
            to = (me.at(axis) + d) % 4
            send(e.a1s[p].at[rows(to * 16, 16)], e.r2s[p].at[d - 1], ssem.at[p], rsem.at[p, 1], me.peer(axis, d))
    drain(e.csem.at[0], e.outs)
    share(SHARES[1])
    for p in range(NP):
        drain(rsem.at[p, 1], e.r2s[p])
        drain(ssem.at[p], e.r2s[p])
        own = e.a1s[p][rows(me.at(ORDERS[p][1]) * 16, 16), :]
        e.a2s[p][...] = (own + e.r2s[p][0]) + (e.r2s[p][1] + e.r2s[p][2])
        axis = ORDERS[p][2]
        for d in (1, 2, 3):
            send(e.a2s[p], e.r3s[p].at[d - 1], ssem.at[p], rsem.at[p, 2], me.peer(axis, d))
    share(SHARES[2])
    for p in range(NP):
        drain(rsem.at[p, 2], e.r3s[p])
        drain(ssem.at[p], e.r3s[p])
        base = me.at(ORDERS[p][0]) * 64 + me.at(ORDERS[p][1]) * 16
        piece = e.fulls[p].at[core, rows(base, 16)]
        piece[...] = (e.a2s[p][...] + e.r3s[p][0]) + (e.r3s[p][1] + e.r3s[p][2])
        axis = ORDERS[p][1]
        for d in (1, 2, 3):
            send(piece, piece, ssem.at[p], rsem.at[p, 3], me.peer(axis, d))
    share(SHARES[3])
    for p in range(NP):
        drain(rsem.at[p, 3], e.r2s[p])
        drain(ssem.at[p], e.r2s[p])
        axis = ORDERS[p][0]
        piece = e.fulls[p].at[core, rows(me.at(axis) * 64, 64)]
        for d in (1, 2, 3):
            send(piece, piece, ssem.at[p], rsem.at[p, 4], me.peer(axis, d))
    s6 = []
    for p in range(NP):
        drain(rsem.at[p, 4], e.r1s[p])
        drain(ssem.at[p], e.r1s[p])
        piece = e.fulls[p].at[core]
        s6.append(send(piece, piece, ssem.at[p], rsem.at[p, 5], mate))
    for p in range(NP):
        s6[p].wait()
    for t in range(0, TOK, 32):
        total = jnp.zeros((32, 1), jnp.float32)
        for p in range(NP):
            for h in range(2):
                v = e.fulls[p][h, pl.ds(t, 32), :].astype(jnp.float32)
                total = total + jnp.sum(v * v, axis=1, keepdims=True)
        scale = lax.rsqrt(total * (1.0 / D) + 1e-05)
        for p, (off, width) in enumerate(PARTS):
            for h in range(2):
                v = e.fulls[p][h, pl.ds(t, 32), :].astype(jnp.float32)
                cols = pl.ds(h * HALF + off, width)
                e.x[pl.ds(t, 32), cols] = (v * scale * gain_ref[:, cols]).astype(jnp.bfloat16)

    def client_block(q):
        start, width = SPANS[q]
        for k in range(2):
            wload[q, k].wait()
        if q < 3:
            g = jnp.dot(e.x[...], e.w[q * 2], preferred_element_type=jnp.float32)
            u = jnp.dot(e.x[...], e.w[q * 2 + 1], preferred_element_type=jnp.float32)
        else:
            both = jnp.dot(e.x[...], e.w[6], preferred_element_type=jnp.float32)
            g, u = both[:, :128], both[:, 128:]
        cols = pl.ds(start, width)
        e.units[0, :, cols] = spread(gated(g, u), 0)
        mine = e.units.at[0, :, cols]
        send(mine, e.units.at[1, :, cols], e.zs.at[0], e.zr.at[(0, 2, 2, 1)[q]], me.peer("z", 1))
        send(mine, e.units.at[3, :, cols], e.zs.at[0], e.zr.at[(5, 3, 4, 5)[q]], me.peer("z", 3))

    def relay(q):
        slot, step = (1, 1) if q in (0, 3) else (3, 3)
        piece = e.units.at[slot, :, pl.ds(*SPANS[q])]
        drain(e.zr.at[(0, 3, 4, 1)[q]], piece)
        send(piece, e.units.at[2, :, pl.ds(*SPANS[q])], e.zs.at[1], e.zr.at[6], me.peer("z", step))

    client_block(0)
    drain(e.wshare.at[0], e.wr.at[:, pl.ds(256, D - 256)])
    drain(e.wshare.at[1], e.wr.at[:, pl.ds(256, D - 256)])
    e.swap[...] = lax.dot_general(e.wr[...], e.x[...], (((1,), (1,)), ((), ())), preferred_element_type=jnp.float32)
    c3 = send(e.swap, e.swin, e.csem.at[1], e.crsem.at[4], mate)

    client_block(1)
    c3.wait()
    mine = e.swap[...]
    theirs = e.swin[...]
    lead = core == 0
    g = jnp.where(lead, mine, theirs)
    u = jnp.where(lead, theirs, mine)
    high = me.y // 2
    piece_rows = rows(high * FF_HERE + here * PIECE, PIECE)
    half = pl.ds(pl.multiple_of(core * 128, 128), 128)
    piece_std = spread(gated(g, u), 1)
    e.refs[piece_rows, half] = jnp.where(lead, piece_std[:, :128], piece_std[:, 128:])
    piece = e.refs.at[piece_rows, half]

    for dx, f in RING8:
        send(piece, piece, e.xs.at[0], e.xr.at[0], me.plane_peer(dx, f, 0))
    send(piece, piece, e.xs.at[1], e.xr.at[1], me.plane_peer(0, 0, 1))
    client_block(2)
    client_block(3)
    piece = e.refs.at[rows((1 - high) * FF_HERE + here * PIECE, PIECE), half]
    drain(e.xr.at[1], piece)
    drain(e.xs.at[1], piece)
    for dx, f in RING8:
        send(piece, piece, e.xs.at[1], e.xr.at[2], me.plane_peer(dx, f, 0))

    def ref_arrived(k):
        seven = e.refs.at[pl.ds(0, 7 * PIECE), half]
        drain(e.xr.at[(0, 2)[k]], seven)
        drain(e.xs.at[k], seven)
        block = high if k == 0 else 1 - high
        part = e.refs.at[rows(block * FF_HERE, FF_HERE), half]
        return send(part, part, e.csem.at[2 + k], e.crsem.at[5 + k], mate)

    def align(slot, first, block):
        @pl.loop(0, FF_HERE // JC)
        def _(t):
            js = rows(block * FF_HERE + t * JC, JC)
            r = e.refs[js, :]
            a = jnp.zeros((JC, 128), jnp.float32) if first else e.cs[js, :]
            b = jnp.zeros((JC, 128), jnp.float32) if first else e.ws[js, :]
            for start, width in SPANS:
                s = jnp.dot(r, e.units[slot, :, pl.ds(start, width)], preferred_element_type=jnp.float32)
                v = jnp.exp2(s * EXP_SCALE)
                e.wts[:, pl.ds(start, width)] = v.astype(jnp.bfloat16)
                vs = v * s
                for o in range(0, width, 128):
                    a = a + v[:, o : o + 128]
                    b = b + vs[:, o : o + 128]
            e.cs[js, :] = a
            e.ws[js, :] = b
            got = lax.dot_general(
                e.wts[...], e.units[slot], (((1,), (1,)), ((), ())), preferred_element_type=jnp.float32
            )
            e.num[js, :] = got if first else e.num[js, :] + got

    def to_row(v):
        return jnp.sum(jnp.where(eye, jnp.sum(v, axis=1, keepdims=True), 0.0), axis=0, keepdims=True)

    def join_start():
        for block in range(2):
            for q in range(7):
                js = pl.ds(block * FF_HERE + q * 128, 128)
                e.col[block, pl.ds(q, 1), :] = to_row(e.cs[js, :])
                e.col[block, pl.ds(q + 8, 1), :] = to_row(e.ws[js, :])
        return send(e.col, e.colin, e.csem.at[4], e.crsem.at[7], me.peer("y", 2))

    def normalize(block):
        for q in range(7):
            js = pl.ds(block * FF_HERE + q * 128, 128)
            inv = 1.0 / (e.col[block, pl.ds(q, 1), :] + e.colin[block, pl.ds(q, 1), :])
            inv = jnp.sum(jnp.where(eye, inv, 0.0), axis=1, keepdims=True)
            n = (e.num[js, :] * inv).astype(jnp.bfloat16)
            e.nout[0, js, :] = n[:, :128]
            e.nout[1, js, :] = n[:, 128:]
        bs = pl.ds(block * FF_HERE, FF_HERE)
        return send(e.nout.at[other, bs], e.nin.at[bs], e.csem.at[5 + block], e.crsem.at[8 + block], mate)

    def reduce_start(block):
        bs = pl.ds(block * FF_HERE, FF_HERE)
        e.nsum[bs, :] = e.nout[core, bs, :] + e.nin[bs, :]
        hop = (block + high) % 2
        for dx in range(4):
            for f in range(2):
                n = hop * 8 + dx * 2 + f
                src = e.nsum.at[rows(block * FF_HERE + me.plane_piece(dx, f) * PIECE, PIECE)]
                copy = pltpu.make_async_remote_copy(
                    src_ref=src, dst_ref=e.f2.at[n], send_sem=e.xs.at[2], recv_sem=e.xr.at[3],
                    device_id=me.plane_peer(dx, f, hop), device_id_type=MESH,
                )
                if dx == 0 and f == 0:
                    pl.when(hop != 0)(copy.start)
                else:
                    copy.start()

    c5 = ref_arrived(0)
    relay(0)
    c5.wait()
    align(0, True, high)
    relay(1)
    c5 = ref_arrived(1)
    relay(2)
    c5.wait()
    align(0, True, 1 - high)
    relay(3)
    drain(e.zr.at[2], e.units.at[1, :, pl.ds(256, 512)])
    align(1, False, 0)
    align(1, False, 1)
    drain(e.zr.at[5], e.units.at[3, :, pl.ds(0, 384)])
    align(3, False, 0)
    align(3, False, 1)
    drain(e.zr.at[6], e.units.at[2])
    align(2, False, 0)
    align(2, False, 1)
    c6 = join_start()
    c6.wait()
    c7 = [normalize(0), normalize(1)]
    for q in range(7):
        below = e.col[high, pl.ds(q, 1), :] + e.colin[high, pl.ds(q, 1), :]
        above = e.col[high, pl.ds(q + 8, 1), :] + e.colin[high, pl.ds(q + 8, 1), :]
        score_ref[:, pl.ds(q * 128, 128)] = above / below * (1.0 / TOK)
    for block in range(2):
        c7[block].wait()
        reduce_start(block)
    drain(e.xr.at[3], e.f2.at[pl.ds(1, 15)])
    drain(e.xs.at[2], e.f2.at[pl.ds(1, 15)])
    total = e.nsum[piece_rows, :].astype(jnp.float32)
    for n in range(1, 16):
        total = total + e.f2[n].astype(jnp.float32)
    mine = e.fin.at[core, here]
    mine[...] = total.astype(jnp.bfloat16)
    for dx, f in RING8:
        send(mine, mine, e.xs.at[3], e.xr.at[4], me.plane_peer(dx, f, 0))
    drain(e.xr.at[4], e.fin.at[0, pl.ds(1, 7)])
    drain(e.xs.at[3], e.fin.at[0, pl.ds(1, 7)])
    c10 = send(e.fin.at[core], e.fin.at[core], e.csem.at[7], e.crsem.at[10], mate)
    for _ in range(2):
        drain(e.zs.at[0], e.units.at[0])
    drain(e.zs.at[1], e.units.at[2])
    c10.wait()
    fin_ref[...] = e.fin[...]


def finish_kernel(fin_ref, mean_ref, merged_ref, score_ref):
    for s in range(8):
        for h in range(2):
            merged_ref[pl.ds(s * PIECE, PIECE), pl.ds(h * 128, 128)] = fin_ref[h, s].astype(jnp.float32) * (1.0 / 16)
    score_ref[...] = mean_ref[...]


def layout():
    bf, f32 = jnp.bfloat16, jnp.float32
    dma = pltpu.SemaphoreType.DMA
    vm = pltpu.VMEM
    widths = [w for _, w in PARTS]
    return {
        "tabs": vm((8, 512, 512), bf),
        "accs": vm((TOK, HALF), bf),
        "outs": vm((TOK, HALF), bf),
        "cins": vm((TOK, HALF), bf),
        "r1s": [vm((3, 64, w), bf) for w in widths],
        "a1s": [vm((64, w), bf) for w in widths],
        "r2s": [vm((3, 16, w), bf) for w in widths],
        "a2s": [vm((16, w), bf) for w in widths],
        "r3s": [vm((3, 16, w), bf) for w in widths],
        "fulls": [vm((2, TOK, w), bf) for w in widths],
        "pick": vm((TOK, 512), bf),
        "x": vm((TOK, D), bf),
        "w": vm((7, D, 256), bf),
        "rw": vm((2, 256, FF_HERE), bf),
        "rt": vm((2, FF_HERE, 256), bf),
        "wr": vm((PIECE, D), bf),
        "swap": vm((PIECE, TOK), f32),
        "swin": vm((PIECE, TOK), f32),
        "refs": vm((JOINT, TOK), bf),
        "units": vm((4, TOK, FF_HERE), bf),
        "wts": vm((JC, FF_HERE), bf),
        "num": vm((JOINT, TOK), f32),
        "cs": vm((JOINT, 128), f32),
        "ws": vm((JOINT, 128), f32),
        "col": vm((2, 16, 128), f32),
        "colin": vm((2, 16, 128), f32),
        "nout": vm((2, JOINT, 128), bf),
        "nin": vm((JOINT, 128), bf),
        "nsum": vm((JOINT, 128), bf),
        "f2": vm((16, PIECE, 128), bf),
        "fin": vm((2, 8, PIECE, 128), bf),
        "tsem": dma((8,)),
        "ssem": dma((NP,)),
        "rsem": dma((NP, 6)),
        "wsem": dma((8,)),
        "rwsem": dma((1,)),
        "wshare": dma((2,)),
        "csem": dma((8,)),
        "crsem": dma((11,)),
        "zs": dma((2,)),
        "zr": dma((7,)),
        "xs": dma((4,)),
        "xr": dma((5,)),
    }


class Refs:
    def __init__(self, scratch):
        left = list(scratch)
        for name, shape in layout().items():
            if isinstance(shape, list):
                setattr(self, name, [left.pop(0) for _ in shape])
            else:
                setattr(self, name, left.pop(0))


def body(token_ids, embed_table, norm_gain, client_gate, client_up, ref_gate, ref_up):
    shapes = []
    for shape in layout().values():
        shapes += shape if isinstance(shape, list) else [shape]
    vmem = pl.BlockSpec(memory_space=pltpu.VMEM)
    hbm = pl.BlockSpec(memory_space=pl.ANY)
    f32 = jnp.float32
    fin, mean = pl.pallas_call(
        kernel,
        out_shape=(
            jax.ShapeDtypeStruct((2, 8, PIECE, 128), jnp.bfloat16),
            jax.ShapeDtypeStruct((1, FF_HERE), f32),
        ),
        in_specs=[vmem, vmem, hbm, hbm, hbm, hbm, hbm],
        out_specs=(vmem, vmem),
        scratch_shapes=shapes,
        compiler_params=pltpu.CompilerParams(collective_id=0, has_side_effects=True, vmem_limit_bytes=60 << 20),
        name="soft_alignment",
    )(token_ids[None, :], norm_gain[None, :], embed_table, client_gate, client_up, ref_gate, ref_up)
    return pl.pallas_call(
        finish_kernel,
        out_shape=(jax.ShapeDtypeStruct((FF_HERE, TOK), f32), jax.ShapeDtypeStruct((1, FF_HERE), f32)),
        in_specs=[vmem, vmem],
        out_specs=(vmem, vmem),
        name="finish",
    )(fin, mean)


def solution(mesh):
    in_specs = (
        P(),
        P(("client", "unit"), None),
        P(),
        P("client", None, "unit"),
        P("client", None, "unit"),
        P("client", "unit"),
        P("client", "unit"),
    )
    out_specs = (P("unit", None), P("client", "unit"))
    return jax.shard_map(body, mesh=mesh, in_specs=in_specs, out_specs=out_specs, check_vma=False)
```

```python
import jax
import jax.numpy as jnp
from jax import lax
from jax.experimental import pallas as pl
from jax.experimental.pallas import tpu as pltpu
from jax.sharding import PartitionSpec as P

sharpness = 40.0
MESH = pl.DeviceIdType.MESH

TOK = 256
D = 4096
HALF = D // 2
PARTS = ((0, 384), (384, 384), (768, 384), (1152, 384), (1536, 256), (1792, 256))
ORDERS = ("xyz", "yzx", "zxy") * 2
NP = len(PARTS)


class Place:
    def __init__(self):
        client = lax.axis_index("client")
        unit = lax.axis_index("unit")
        self.core = client % 2
        self.x = (client // 2) % 4
        self.y = (unit % 2) * 2 + client // 8
        self.z = unit // 2

    def at(self, axis):
        return getattr(self, axis)

    def peer(self, axis, step):
        x, y, z, core = self.x, self.y, self.z, self.core
        if axis == "x":
            x = (x + step) % 4
        elif axis == "y":
            y = (y + step) % 4
        elif axis == "z":
            z = (z + step) % 4
        else:
            core = 1 - core
        return {"client": (y % 2) * 8 + x * 2 + core, "unit": z * 2 + y // 2}


    def plane_peer(self, dx, flip, hflip, cflip=0):
        x = (self.x + dx) % 4
        low = (self.y % 2 + flip) % 2
        high = (self.y // 2 + hflip) % 2
        return {"client": low * 8 + x * 2 + (self.core + cflip) % 2, "unit": self.z * 2 + high}

    def plane_piece(self, dx, flip):
        return ((self.x + dx) % 4) * 2 + (self.y % 2 + flip) % 2


def send(src, dst, ssem, rsem, peer):
    copy = pltpu.make_async_remote_copy(
        src_ref=src, dst_ref=dst, send_sem=ssem, recv_sem=rsem, device_id=peer, device_id_type=MESH
    )
    copy.start()
    return copy


def drain(sem, ref):
    pltpu.make_async_copy(ref, ref, sem).wait()


def rows(start, size):
    return pl.ds(pl.multiple_of(start, size), size)

FF_HERE = 896
PIECE = 112
JOINT = 2 * FF_HERE
SHARES = (4, 3, 3, 3, 2, 0)
SPANS = ((0, 256), (256, 256), (512, 256), (768, 128))
RING8 = [(dx, f) for dx in range(4) for f in range(2)][1:]
CROSS = [(dx, f, c) for dx in range(4) for f in range(2) for c in range(2)][1:]
RING16 = [(dx, f, h) for h in range(2) for dx in range(4) for f in range(2)][1:]
EXP_SCALE = sharpness / TOK * 1.4426950408889634


def spread(h, axis):
    center = jnp.mean(h, axis=axis, keepdims=True)
    shifted = h - center
    width = jnp.sqrt(jnp.mean(shifted * shifted, axis=axis, keepdims=True) + 1e-06)
    return (shifted / width).astype(jnp.bfloat16)


def gated(g, u):
    return g / (1.0 + jnp.exp(-g)) * u


def kernel(ids_ref, gain_ref, table_ref, cg_ref, cu_ref, rg_ref, ru_ref, fin_ref, score_ref, *scratch):
    e = Refs(scratch)
    me = Place()
    core, other = me.core, 1 - me.core
    mate = me.peer("core", 1)
    client = lax.axis_index("client")
    ssem, rsem = e.ssem, e.rsem

    def table_load(k):
        half = other if k < 4 else core
        at = pl.multiple_of(half * HALF + k % 4 * 512, 512)
        load = pltpu.make_async_copy(table_ref.at[:, pl.ds(at, 512)], e.tabs.at[k], e.tsem.at[k])
        load.start()
        return load

    loads = [table_load(k) for k in range(4)]
    for t, src in enumerate((rg_ref, ru_ref)):
        pltpu.make_async_copy(src, e.rw.at[t], e.rwsem.at[0]).start()
    loads += [table_load(k) for k in range(4, 8)]

    barrier = pltpu.get_barrier_semaphore()
    peers = [me.plane_peer(*r) for r in RING16] + [me.peer("z", d) for d in (1, 2, 3)] + [mate]
    peers += [me.plane_peer(dx, f, 0, 1) for dx, f in RING8]
    for peer in peers:
        pl.semaphore_signal(barrier, inc=1, device_id=peer, device_id_type=MESH)

    eye = lax.broadcasted_iota(jnp.int32, (128, 128), 0) == lax.broadcasted_iota(jnp.int32, (128, 128), 1)
    start = (client * 8 + lax.axis_index("unit")) * 512
    table_rows = (start + lax.broadcasted_iota(jnp.int32, (1, 512), 1)).astype(jnp.float32)
    for t in range(2):
        wide = ids_ref[:, pl.ds(t * 128, 128)].astype(jnp.float32)
        tall = jnp.sum(jnp.where(eye, wide, 0.0), axis=1, keepdims=True)
        e.pick[pl.ds(t * 128, 128), :] = jnp.where(tall == table_rows, 1.0, 0.0).astype(jnp.bfloat16)

    def looked_up(k):
        loads[k].wait()
        return jnp.dot(e.pick[...], e.tabs[k], preferred_element_type=jnp.float32).astype(jnp.bfloat16)

    chunks = [pl.ds(k * 512, 512) for k in range(4)]
    for k in range(4):
        e.outs[:, chunks[k]] = looked_up(k)
    here = me.plane_piece(0, 0)
    depth = pl.ds(pl.multiple_of(client * 256, 256), 256)
    drain(e.rwsem.at[0], e.rw)
    for t in range(2):
        e.rt[t] = e.rw[t].T
    e.wr[:, depth] = e.rt[core, rows(here * PIECE, PIECE), :]
    shared = []

    def share(count):
        for _ in range(count):
            n = len(shared)
            dx, f, c = CROSS[n]
            src = e.rt.at[(core + c) % 2, rows(me.plane_piece(dx, f) * PIECE, PIECE)]
            shared.append(send(src, e.wr.at[:, depth], e.wshare.at[0], e.wshare.at[1], me.plane_peer(dx, f, 0, c)))

    pl.semaphore_wait(barrier, len(peers))
    sent = []
    for k in range(4):
        sent.append(send(e.outs.at[:, chunks[k]], e.cins.at[:, chunks[k]], e.csem.at[0], e.crsem.at[k], mate))
    share(SHARES[0])
    for k in range(4):
        e.accs[:, chunks[k]] = looked_up(4 + k)
    wload = {}
    for q in range(3):
        for k, src in enumerate((cg_ref, cu_ref)):
            load = pltpu.make_async_copy(
                src.at[0, :, pl.ds(q * 256, 256)], e.w.at[q * 2 + k], e.wsem.at[q * 2 + k]
            )
            load.start()
            wload[q, k] = load
    for k, src in enumerate((cg_ref, cu_ref)):
        load = pltpu.make_async_copy(
            src.at[0, :, pl.ds(768, 128)], e.w.at[6, :, pl.ds(k * 128, 128)], e.wsem.at[6 + k]
        )
        load.start()
        wload[3, k] = load

    for k in range(4):
        sent[k].wait_recv()
        e.accs[:, chunks[k]] = e.accs[:, chunks[k]] + e.cins[:, chunks[k]]
    for p in range(NP):
        axis = ORDERS[p][0]
        for d in (1, 2, 3):
            to = (me.at(axis) + d) % 4
            src = e.accs.at[rows(to * 64, 64), pl.ds(*PARTS[p])]
            send(src, e.r1s[p].at[d - 1], ssem.at[p], rsem.at[p, 0], me.peer(axis, d))

    share(SHARES[1])
    for p in range(NP):
        drain(rsem.at[p, 0], e.r1s[p])
        drain(ssem.at[p], e.r1s[p])
        own = e.accs[rows(me.at(ORDERS[p][0]) * 64, 64), pl.ds(*PARTS[p])]
        e.a1s[p][...] = (own + e.r1s[p][0]) + (e.r1s[p][1] + e.r1s[p][2])
        axis = ORDERS[p][1]
        for d in (1, 2, 3):
            to = (me.at(axis) + d) % 4
            send(e.a1s[p].at[rows(to * 16, 16)], e.r2s[p].at[d - 1], ssem.at[p], rsem.at[p, 1], me.peer(axis, d))
    drain(e.csem.at[0], e.outs)
    share(SHARES[2])
    for p in range(NP):
        drain(rsem.at[p, 1], e.r2s[p])
        drain(ssem.at[p], e.r2s[p])
        own = e.a1s[p][rows(me.at(ORDERS[p][1]) * 16, 16), :]
        e.a2s[p][...] = (own + e.r2s[p][0]) + (e.r2s[p][1] + e.r2s[p][2])
        axis = ORDERS[p][2]
        for d in (1, 2, 3):
            send(e.a2s[p], e.r3s[p].at[d - 1], ssem.at[p], rsem.at[p, 2], me.peer(axis, d))
    share(SHARES[3])
    for p in range(NP):
        drain(rsem.at[p, 2], e.r3s[p])
        drain(ssem.at[p], e.r3s[p])
        base = me.at(ORDERS[p][0]) * 64 + me.at(ORDERS[p][1]) * 16
        piece = e.fulls[p].at[core, rows(base, 16)]
        piece[...] = (e.a2s[p][...] + e.r3s[p][0]) + (e.r3s[p][1] + e.r3s[p][2])
        axis = ORDERS[p][1]
        for d in (1, 2, 3):
            send(piece, piece, ssem.at[p], rsem.at[p, 3], me.peer(axis, d))
    share(SHARES[4])
    for p in range(NP):
        drain(rsem.at[p, 3], e.r2s[p])
        drain(ssem.at[p], e.r2s[p])
        axis = ORDERS[p][0]
        piece = e.fulls[p].at[core, rows(me.at(axis) * 64, 64)]
        for d in (1, 2, 3):
            send(piece, piece, ssem.at[p], rsem.at[p, 4], me.peer(axis, d))
    share(SHARES[5])
    s6 = []
    for p in range(NP):
        drain(rsem.at[p, 4], e.r1s[p])
        drain(ssem.at[p], e.r1s[p])
        piece = e.fulls[p].at[core]
        s6.append(send(piece, piece, ssem.at[p], rsem.at[p, 5], mate))
    apart = e.wr.at[:, pl.ds(256, D - 256)]
    drain(e.wshare.at[1], apart)
    drain(e.wshare.at[0], apart)
    for t in range(0, D, 512):
        cols = pl.ds(t, 512)
        e.wr[:, cols] = (e.wr[:, cols].astype(jnp.float32) * gain_ref[:, cols]).astype(jnp.bfloat16)

    def ref_part(p, h):
        off, width = PARTS[p]
        cols = pl.ds(pl.multiple_of(h * HALF + off, 128), width)
        return lax.dot_general(
            e.wr[:, cols], e.fulls[p][h], (((1,), (1,)), ((), ())), preferred_element_type=jnp.float32
        )

    product = ref_part(0, core)
    for p in range(1, NP):
        product = product + ref_part(p, core)
    for p in range(NP):
        s6[p].wait()
        product = product + ref_part(p, other)
    e.swap[...] = product
    c3 = send(e.swap, e.swin, e.csem.at[1], e.crsem.at[4], mate)
    for t in range(0, TOK, 32):
        total = jnp.zeros((32, 1), jnp.float32)
        for p in range(NP):
            for h in range(2):
                v = e.fulls[p][h, pl.ds(t, 32), :].astype(jnp.float32)
                total = total + jnp.sum(v * v, axis=1, keepdims=True)
        scale = lax.rsqrt(total * (1.0 / D) + 1e-05)
        e.scl[pl.ds(t, 32), :] = jnp.broadcast_to(scale, (32, 128))
        for p, (off, width) in enumerate(PARTS):
            for h in range(2):
                v = e.fulls[p][h, pl.ds(t, 32), :].astype(jnp.float32)
                cols = pl.ds(h * HALF + off, width)
                e.x[pl.ds(t, 32), cols] = (v * scale * gain_ref[:, cols]).astype(jnp.bfloat16)

    c3.wait()
    scale_row = jnp.concatenate(
        [jnp.sum(jnp.where(eye, e.scl[pl.ds(t, 128), :], 0.0), axis=0, keepdims=True) for t in (0, 128)], axis=1
    )
    mine = e.swap[...] * scale_row
    theirs = e.swin[...] * scale_row
    lead = core == 0
    g = jnp.where(lead, mine, theirs)
    u = jnp.where(lead, theirs, mine)
    high = me.y // 2
    piece_rows = rows(high * FF_HERE + here * PIECE, PIECE)
    half = pl.ds(pl.multiple_of(core * 128, 128), 128)
    piece_std = spread(gated(g, u), 1)
    e.refs[piece_rows, half] = jnp.where(lead, piece_std[:, :128], piece_std[:, 128:])
    piece = e.refs.at[piece_rows, half]
    for dx, f in RING8:
        send(piece, piece, e.xs.at[0], e.xr.at[0], me.plane_peer(dx, f, 0))
    for dx in range(4):
        for f in range(2):
            send(piece, piece, e.xs.at[1], e.xr.at[2], me.plane_peer(dx, f, 1))

    def client_block(q):
        start, width = SPANS[q]
        for k in range(2):
            wload[q, k].wait()
        if q < 3:
            g = jnp.dot(e.x[...], e.w[q * 2], preferred_element_type=jnp.float32)
            u = jnp.dot(e.x[...], e.w[q * 2 + 1], preferred_element_type=jnp.float32)
        else:
            both = jnp.dot(e.x[...], e.w[6], preferred_element_type=jnp.float32)
            g, u = both[:, :128], both[:, 128:]
        cols = pl.ds(start, width)
        e.units[0, :, cols] = spread(gated(g, u), 0)
        mine = e.units.at[0, :, cols]
        send(mine, e.units.at[1, :, cols], e.zs.at[0], e.zr.at[q], me.peer("z", 1))
        send(mine, e.units.at[3, :, cols], e.zs.at[0], e.zr.at[8 + q], me.peer("z", 3))

    def relay(q):
        slot, step = (1, 1) if q in (0, 3) else (3, 3)
        piece = e.units.at[slot, :, pl.ds(*SPANS[q])]
        drain(e.zr.at[q if slot == 1 else 8 + q], piece)
        send(piece, e.units.at[2, :, pl.ds(*SPANS[q])], e.zs.at[1], e.zr.at[4 + q], me.peer("z", step))

    def unit_wait(slot, q):
        drain(e.zr.at[(slot - 1) * 4 + q], e.units.at[slot, :, pl.ds(*SPANS[q])])

    client_block(0)
    client_block(1)
    client_block(2)
    client_block(3)
    def ref_arrived(k):
        came = e.refs.at[pl.ds(0, (7 + k) * PIECE), half]
        drain(e.xr.at[(0, 2)[k]], came)
        drain(e.xs.at[k], came)
        block = high if k == 0 else 1 - high
        part = e.refs.at[rows(block * FF_HERE, FF_HERE), half]
        return send(part, part, e.csem.at[2 + k], e.crsem.at[5 + k], mate)

    def align(slot, block, k, first=False):
        left, wide = ((0, 512), (512, 384))[k]
        js = rows(block * FF_HERE, FF_HERE)
        r = e.refs[js, :]
        a = jnp.zeros((FF_HERE, 128), jnp.float32) if first else e.cs[js, :]
        b = jnp.zeros((FF_HERE, 128), jnp.float32) if first else e.ws[js, :]
        for start in range(0, wide, 256):
            width = min(256, wide - start)
            s = jnp.dot(r, e.units[slot, :, pl.ds(left + start, width)], preferred_element_type=jnp.float32)
            v = jnp.exp2(s * EXP_SCALE)
            e.wts[:, pl.ds(start, width)] = v.astype(jnp.bfloat16)
            vs = v * s
            for o in range(0, width, 128):
                a = a + v[:, o : o + 128]
                b = b + vs[:, o : o + 128]
        e.cs[js, :] = a
        e.ws[js, :] = b
        got = lax.dot_general(
            e.wts[:, pl.ds(0, wide)], e.units[slot, :, pl.ds(left, wide)], (((1,), (1,)), ((), ())),
            preferred_element_type=jnp.float32,
        )
        e.num[js, :] = got if first else e.num[js, :] + got

    def to_row(v):
        return jnp.sum(jnp.where(eye, jnp.sum(v, axis=1, keepdims=True), 0.0), axis=0, keepdims=True)

    def join_start(block):
        for q in range(7):
            js = pl.ds(block * FF_HERE + q * 128, 128)
            e.col[block, pl.ds(q, 1), :] = to_row(e.cs[js, :])
            e.col[block, pl.ds(q + 8, 1), :] = to_row(e.ws[js, :])
        return send(e.col.at[block], e.colin.at[block], e.jsem.at[block], e.jsem.at[2 + block], me.peer("y", 2))

    def normalize(block):
        for q in range(7):
            js = pl.ds(block * FF_HERE + q * 128, 128)
            inv = 1.0 / (e.col[block, pl.ds(q, 1), :] + e.colin[block, pl.ds(q, 1), :])
            inv = jnp.sum(jnp.where(eye, inv, 0.0), axis=1, keepdims=True)
            n = (e.num[js, :] * inv).astype(jnp.bfloat16)
            e.nout[0, js, :] = n[:, :128]
            e.nout[1, js, :] = n[:, 128:]
        bs = pl.ds(block * FF_HERE, FF_HERE)
        return send(e.nout.at[other, bs], e.nin.at[bs], e.csem.at[5 + block], e.crsem.at[8 + block], mate)

    def reduce_start(block):
        bs = pl.ds(block * FF_HERE, FF_HERE)
        e.nsum[bs, :] = e.nout[core, bs, :] + e.nin[bs, :]
        hop = (block + high) % 2
        for dx in range(4):
            for f in range(2):
                n = hop * 8 + dx * 2 + f
                src = e.nsum.at[rows(block * FF_HERE + me.plane_piece(dx, f) * PIECE, PIECE)]
                copy = pltpu.make_async_remote_copy(
                    src_ref=src, dst_ref=e.f2.at[n], send_sem=e.xs.at[2], recv_sem=e.xr.at[3],
                    device_id=me.plane_peer(dx, f, hop), device_id_type=MESH,
                )
                if dx == 0 and f == 0:
                    pl.when(hop != 0)(copy.start)
                else:
                    copy.start()

    c5 = ref_arrived(0)
    relay(0)
    c5.wait()
    align(0, high, 0, True)
    align(0, high, 1)
    c5 = ref_arrived(1)
    relay(1)
    c5.wait()
    align(0, 1 - high, 0, True)
    align(0, 1 - high, 1)
    unit_wait(1, 1)
    unit_wait(3, 0)
    align(1, 0, 0)
    align(3, 0, 0)
    relay(2)
    align(1, 1, 0)
    align(3, 1, 0)
    relay(3)
    unit_wait(1, 2)
    unit_wait(3, 3)
    align(1, 0, 1)
    align(3, 0, 1)
    align(1, 1, 1)
    align(3, 1, 1)
    unit_wait(2, 0)
    unit_wait(2, 1)
    align(2, 0, 0)
    align(2, 1, 0)
    unit_wait(2, 3)
    unit_wait(2, 2)
    align(2, 0, 1)
    c6 = join_start(0)
    align(2, 1, 1)
    c61 = join_start(1)
    c6.wait()
    c7 = [normalize(0)]
    c7[0].wait()
    reduce_start(0)
    c61.wait()
    c7 = [normalize(1)]
    for q in range(7):
        below = e.col[high, pl.ds(q, 1), :] + e.colin[high, pl.ds(q, 1), :]
        above = e.col[high, pl.ds(q + 8, 1), :] + e.colin[high, pl.ds(q + 8, 1), :]
        score_ref[:, pl.ds(q * 128, 128)] = above / below * (1.0 / TOK)
    c7[0].wait()
    reduce_start(1)
    drain(e.xr.at[3], e.f2.at[pl.ds(1, 15)])
    drain(e.xs.at[2], e.f2.at[pl.ds(1, 15)])
    total = e.nsum[piece_rows, :].astype(jnp.float32)
    for n in range(1, 16):
        total = total + e.f2[n].astype(jnp.float32)
    mine = e.fin.at[core, here]
    mine[...] = total.astype(jnp.bfloat16)
    for dx, f in RING8:
        send(mine, mine, e.xs.at[3], e.xr.at[4], me.plane_peer(dx, f, 0))
    drain(e.xr.at[4], e.fin.at[0, pl.ds(1, 7)])
    drain(e.xs.at[3], e.fin.at[0, pl.ds(1, 7)])
    c10 = send(e.fin.at[core], e.fin.at[core], e.csem.at[7], e.crsem.at[10], mate)
    for _ in range(2):
        drain(e.zs.at[0], e.units.at[0])
    drain(e.zs.at[1], e.units.at[2])
    c10.wait()
    fin_ref[...] = e.fin[...]


def finish_kernel(fin_ref, mean_ref, merged_ref, score_ref):
    for s in range(8):
        for h in range(2):
            merged_ref[pl.ds(s * PIECE, PIECE), pl.ds(h * 128, 128)] = fin_ref[h, s].astype(jnp.float32) * (1.0 / 16)
    score_ref[...] = mean_ref[...]


def layout():
    bf, f32 = jnp.bfloat16, jnp.float32
    dma = pltpu.SemaphoreType.DMA
    vm = pltpu.VMEM
    widths = [w for _, w in PARTS]
    return {
        "tabs": vm((8, 512, 512), bf),
        "accs": vm((TOK, HALF), bf),
        "outs": vm((TOK, HALF), bf),
        "cins": vm((TOK, HALF), bf),
        "r1s": [vm((3, 64, w), bf) for w in widths],
        "a1s": [vm((64, w), bf) for w in widths],
        "r2s": [vm((3, 16, w), bf) for w in widths],
        "a2s": [vm((16, w), bf) for w in widths],
        "r3s": [vm((3, 16, w), bf) for w in widths],
        "fulls": [vm((2, TOK, w), bf) for w in widths],
        "pick": vm((TOK, 512), bf),
        "x": vm((TOK, D), bf),
        "w": vm((7, D, 256), bf),
        "rw": vm((2, 256, FF_HERE), bf),
        "rt": vm((2, FF_HERE, 256), bf),
        "wr": vm((PIECE, D), bf),
        "scl": vm((TOK, 128), f32),
        "swap": vm((PIECE, TOK), f32),
        "swin": vm((PIECE, TOK), f32),
        "refs": vm((JOINT, TOK), bf),
        "units": vm((4, TOK, FF_HERE), bf),
        "wts": vm((FF_HERE, 512), bf),
        "num": vm((JOINT, TOK), f32),
        "cs": vm((JOINT, 128), f32),
        "ws": vm((JOINT, 128), f32),
        "col": vm((2, 16, 128), f32),
        "colin": vm((2, 16, 128), f32),
        "nout": vm((2, JOINT, 128), bf),
        "nin": vm((JOINT, 128), bf),
        "nsum": vm((JOINT, 128), bf),
        "f2": vm((16, PIECE, 128), bf),
        "fin": vm((2, 8, PIECE, 128), bf),
        "tsem": dma((8,)),
        "ssem": dma((NP,)),
        "rsem": dma((NP, 6)),
        "wsem": dma((8,)),
        "rwsem": dma((1,)),
        "wshare": dma((2,)),
        "csem": dma((8,)),
        "crsem": dma((11,)),
        "jsem": dma((4,)),
        "zs": dma((2,)),
        "zr": dma((12,)),
        "xs": dma((4,)),
        "xr": dma((5,)),
    }


class Refs:
    def __init__(self, scratch):
        left = list(scratch)
        for name, shape in layout().items():
            if isinstance(shape, list):
                setattr(self, name, [left.pop(0) for _ in shape])
            else:
                setattr(self, name, left.pop(0))


def body(token_ids, embed_table, norm_gain, client_gate, client_up, ref_gate, ref_up):
    shapes = []
    for shape in layout().values():
        shapes += shape if isinstance(shape, list) else [shape]
    vmem = pl.BlockSpec(memory_space=pltpu.VMEM)
    hbm = pl.BlockSpec(memory_space=pl.ANY)
    f32 = jnp.float32
    fin, mean = pl.pallas_call(
        kernel,
        out_shape=(
            jax.ShapeDtypeStruct((2, 8, PIECE, 128), jnp.bfloat16),
            jax.ShapeDtypeStruct((1, FF_HERE), f32),
        ),
        in_specs=[vmem, vmem, hbm, hbm, hbm, hbm, hbm],
        out_specs=(vmem, vmem),
        scratch_shapes=shapes,
        compiler_params=pltpu.CompilerParams(collective_id=0, has_side_effects=True, vmem_limit_bytes=60 << 20),
        name="soft_alignment",
    )(token_ids[None, :], norm_gain[None, :], embed_table, client_gate, client_up, ref_gate, ref_up)
    return pl.pallas_call(
        finish_kernel,
        out_shape=(jax.ShapeDtypeStruct((FF_HERE, TOK), f32), jax.ShapeDtypeStruct((1, FF_HERE), f32)),
        in_specs=[vmem, vmem],
        out_specs=(vmem, vmem),
        name="finish",
    )(fin, mean)


def solution(mesh):
    in_specs = (
        P(),
        P(("client", "unit"), None),
        P(),
        P("client", None, "unit"),
        P("client", None, "unit"),
        P("client", "unit"),
        P("client", "unit"),
    )
    out_specs = (P("unit", None), P("client", "unit"))
    return jax.shard_map(body, mesh=mesh, in_specs=in_specs, out_specs=out_specs, check_vma=False)
```

```python
import jax
import jax.numpy as jnp
from jax import lax
from jax.experimental import pallas as pl
from jax.experimental.pallas import tpu as pltpu
from jax.sharding import PartitionSpec as P

sharpness = 40.0
MESH = pl.DeviceIdType.MESH

TOK = 256
D = 4096
HALF = D // 2
PARTS = ((0, 384), (384, 384), (768, 384), (1152, 384), (1536, 256), (1792, 256))
ORDERS = ("xyz", "yzx", "zxy") * 2
NP = len(PARTS)


class Place:
    def __init__(self):
        client = lax.axis_index("client")
        unit = lax.axis_index("unit")
        self.core = client % 2
        self.x = (client // 2) % 4
        self.y = (unit % 2) * 2 + client // 8
        self.z = unit // 2

    def at(self, axis):
        return getattr(self, axis)

    def peer(self, axis, step):
        x, y, z, core = self.x, self.y, self.z, self.core
        if axis == "x":
            x = (x + step) % 4
        elif axis == "y":
            y = (y + step) % 4
        elif axis == "z":
            z = (z + step) % 4
        else:
            core = 1 - core
        return {"client": (y % 2) * 8 + x * 2 + core, "unit": z * 2 + y // 2}


    def plane_peer(self, dx, flip, hflip, cflip=0):
        x = (self.x + dx) % 4
        low = (self.y % 2 + flip) % 2
        high = (self.y // 2 + hflip) % 2
        return {"client": low * 8 + x * 2 + (self.core + cflip) % 2, "unit": self.z * 2 + high}

    def plane_piece(self, dx, flip):
        return ((self.x + dx) % 4) * 2 + (self.y % 2 + flip) % 2


def send(src, dst, ssem, rsem, peer):
    copy = pltpu.make_async_remote_copy(
        src_ref=src, dst_ref=dst, send_sem=ssem, recv_sem=rsem, device_id=peer, device_id_type=MESH
    )
    copy.start()
    return copy


def drain(sem, ref):
    pltpu.make_async_copy(ref, ref, sem).wait()


def rows(start, size):
    return pl.ds(pl.multiple_of(start, size), size)

FF_HERE = 896
PIECE = 112
JOINT = 2 * FF_HERE
SHARES = (4, 3, 3, 3, 2, 0)
SPANS = ((0, 256), (256, 256), (512, 256), (768, 128))
RING8 = [(dx, f) for dx in range(4) for f in range(2)][1:]
CROSS = [(dx, f, c) for dx in range(4) for f in range(2) for c in range(2)][1:]
RING16 = [(dx, f, h) for h in range(2) for dx in range(4) for f in range(2)][1:]
EXP_SCALE = sharpness / TOK * 1.4426950408889634


def spread(h, axis):
    center = jnp.mean(h, axis=axis, keepdims=True)
    shifted = h - center
    width = jnp.sqrt(jnp.mean(shifted * shifted, axis=axis, keepdims=True) + 1e-06)
    return (shifted / width).astype(jnp.bfloat16)


def gated(g, u):
    return g / (1.0 + jnp.exp(-g)) * u


def kernel(ids_ref, gain_ref, table_ref, cg_ref, cu_ref, rg_ref, ru_ref, fin_ref, score_ref, *scratch):
    e = Refs(scratch)
    me = Place()
    core, other = me.core, 1 - me.core
    mate = me.peer("core", 1)
    client = lax.axis_index("client")
    ssem, rsem = e.ssem, e.rsem

    def table_load(k):
        half = other if k < 4 else core
        at = pl.multiple_of(half * HALF + k % 4 * 512, 512)
        load = pltpu.make_async_copy(table_ref.at[:, pl.ds(at, 512)], e.tabs.at[k], e.tsem.at[k])
        load.start()
        return load

    loads = [table_load(k) for k in range(4)]
    for t, src in enumerate((rg_ref, ru_ref)):
        pltpu.make_async_copy(src, e.rw.at[t], e.rwsem.at[0]).start()
    loads += [table_load(k) for k in range(4, 8)]

    barrier = pltpu.get_barrier_semaphore()
    peers = [me.plane_peer(*r) for r in RING16] + [me.peer("z", d) for d in (1, 2, 3)] + [mate]
    peers += [me.plane_peer(dx, f, 0, 1) for dx, f in RING8]
    for peer in peers:
        pl.semaphore_signal(barrier, inc=1, device_id=peer, device_id_type=MESH)

    eye = lax.broadcasted_iota(jnp.int32, (128, 128), 0) == lax.broadcasted_iota(jnp.int32, (128, 128), 1)
    start = (client * 8 + lax.axis_index("unit")) * 512
    table_rows = (start + lax.broadcasted_iota(jnp.int32, (1, 512), 1)).astype(jnp.float32)
    for t in range(2):
        wide = ids_ref[:, pl.ds(t * 128, 128)].astype(jnp.float32)
        tall = jnp.sum(jnp.where(eye, wide, 0.0), axis=1, keepdims=True)
        e.pick[pl.ds(t * 128, 128), :] = jnp.where(tall == table_rows, 1.0, 0.0).astype(jnp.bfloat16)

    def looked_up(k):
        loads[k].wait()
        return jnp.dot(e.pick[...], e.tabs[k], preferred_element_type=jnp.float32).astype(jnp.bfloat16)

    chunks = [pl.ds(k * 512, 512) for k in range(4)]
    for k in range(4):
        e.outs[:, chunks[k]] = looked_up(k)
    here = me.plane_piece(0, 0)
    depth = pl.ds(pl.multiple_of(client * 256, 256), 256)
    drain(e.rwsem.at[0], e.rw)
    for t in range(2):
        e.rt[t] = e.rw[t].T
    e.wr[:, depth] = e.rt[core, rows(here * PIECE, PIECE), :]
    shared = []

    def share(count):
        for _ in range(count):
            n = len(shared)
            dx, f, c = CROSS[n]
            src = e.rt.at[(core + c) % 2, rows(me.plane_piece(dx, f) * PIECE, PIECE)]
            shared.append(send(src, e.wr.at[:, depth], e.wshare.at[0], e.wshare.at[1], me.plane_peer(dx, f, 0, c)))

    pl.semaphore_wait(barrier, len(peers))
    sent = []
    for k in range(4):
        sent.append(send(e.outs.at[:, chunks[k]], e.cins.at[:, chunks[k]], e.csem.at[0], e.crsem.at[k], mate))
    share(SHARES[0])
    for k in range(4):
        e.accs[:, chunks[k]] = looked_up(4 + k)
    wload = {}
    for q in range(3):
        for k, src in enumerate((cg_ref, cu_ref)):
            load = pltpu.make_async_copy(
                src.at[0, :, pl.ds(q * 256, 256)], e.w.at[q * 2 + k], e.wsem.at[q * 2 + k]
            )
            load.start()
            wload[q, k] = load
    for k, src in enumerate((cg_ref, cu_ref)):
        load = pltpu.make_async_copy(
            src.at[0, :, pl.ds(768, 128)], e.w.at[6, :, pl.ds(k * 128, 128)], e.wsem.at[6 + k]
        )
        load.start()
        wload[3, k] = load

    for k in range(4):
        sent[k].wait_recv()
        e.accs[:, chunks[k]] = e.accs[:, chunks[k]] + e.cins[:, chunks[k]]
    for p in range(NP):
        axis = ORDERS[p][0]
        for d in (1, 2, 3):
            to = (me.at(axis) + d) % 4
            src = e.accs.at[rows(to * 64, 64), pl.ds(*PARTS[p])]
            send(src, e.r1s[p].at[d - 1], ssem.at[p], rsem.at[p, 0], me.peer(axis, d))

    share(SHARES[1])
    for p in range(NP):
        drain(rsem.at[p, 0], e.r1s[p])
        drain(ssem.at[p], e.r1s[p])
        own = e.accs[rows(me.at(ORDERS[p][0]) * 64, 64), pl.ds(*PARTS[p])]
        e.a1s[p][...] = (own + e.r1s[p][0]) + (e.r1s[p][1] + e.r1s[p][2])
        axis = ORDERS[p][1]
        for d in (1, 2, 3):
            to = (me.at(axis) + d) % 4
            send(e.a1s[p].at[rows(to * 16, 16)], e.r2s[p].at[d - 1], ssem.at[p], rsem.at[p, 1], me.peer(axis, d))
    drain(e.csem.at[0], e.outs)
    share(SHARES[2])
    for p in range(NP):
        drain(rsem.at[p, 1], e.r2s[p])
        drain(ssem.at[p], e.r2s[p])
        own = e.a1s[p][rows(me.at(ORDERS[p][1]) * 16, 16), :]
        e.a2s[p][...] = (own + e.r2s[p][0]) + (e.r2s[p][1] + e.r2s[p][2])
        axis = ORDERS[p][2]
        for d in (1, 2, 3):
            send(e.a2s[p], e.r3s[p].at[d - 1], ssem.at[p], rsem.at[p, 2], me.peer(axis, d))
    share(SHARES[3])
    for p in range(NP):
        drain(rsem.at[p, 2], e.r3s[p])
        drain(ssem.at[p], e.r3s[p])
        base = me.at(ORDERS[p][0]) * 64 + me.at(ORDERS[p][1]) * 16
        piece = e.fulls[p].at[core, rows(base, 16)]
        piece[...] = (e.a2s[p][...] + e.r3s[p][0]) + (e.r3s[p][1] + e.r3s[p][2])
        axis = ORDERS[p][1]
        for d in (1, 2, 3):
            send(piece, piece, ssem.at[p], rsem.at[p, 3], me.peer(axis, d))
    share(SHARES[4])
    for p in range(NP):
        drain(rsem.at[p, 3], e.r2s[p])
        drain(ssem.at[p], e.r2s[p])
        axis = ORDERS[p][0]
        piece = e.fulls[p].at[core, rows(me.at(axis) * 64, 64)]
        for d in (1, 2, 3):
            send(piece, piece, ssem.at[p], rsem.at[p, 4], me.peer(axis, d))
    share(SHARES[5])
    def prepare(p, h, first=False):
        off, width = PARTS[p]
        cols = pl.ds(pl.multiple_of(h * HALF + off, 128), width)
        v = e.fulls[p][h].astype(jnp.float32)
        squares = v * v
        total = squares[:, :128]
        for o in range(128, width, 128):
            total = total + squares[:, o : o + 128]
        e.scl[...] = total if first else e.scl[...] + total
        e.x[:, cols] = (v * gain_ref[:, cols]).astype(jnp.bfloat16)

    s6 = []
    for p in range(NP):
        drain(rsem.at[p, 4], e.r1s[p])
        drain(ssem.at[p], e.r1s[p])
        piece = e.fulls[p].at[core]
        s6.append(send(piece, piece, ssem.at[p], rsem.at[p, 5], mate))
        prepare(p, core, p == 0)
    apart = e.wr.at[:, pl.ds(256, D - 256)]
    drain(e.wshare.at[1], apart)
    drain(e.wshare.at[0], apart)

    def half_of(h):
        return pl.ds(pl.multiple_of(h * HALF, HALF), HALF)

    def ref_half(h):
        return lax.dot_general(
            e.wr[:, half_of(h)], e.x[:, half_of(h)], (((1,), (1,)), ((), ())), preferred_element_type=jnp.float32
        )

    def client_half(k, h):
        return jnp.dot(e.x[:, half_of(h)], e.w[k, half_of(h), :], preferred_element_type=jnp.float32)

    e.swap[...] = ref_half(core)
    for k in range(2):
        wload[0, k].wait()
    e.acc[0] = client_half(0, core)
    for p in range(NP):
        s6[p].wait()
        prepare(p, other)
    e.swap[...] = e.swap[...] + ref_half(other)
    c3 = send(e.swap, e.swin, e.csem.at[1], e.crsem.at[4], mate)
    scale = lax.rsqrt(jnp.sum(e.scl[...], axis=1, keepdims=True) * (1.0 / D) + 1e-05)
    e.scl[...] = jnp.broadcast_to(scale, (TOK, 128))

    def client_block(q):
        start, width = SPANS[q]
        for k in range(2):
            if q > 0:
                wload[q, k].wait()
        if q == 0:
            g = e.acc[0] + client_half(0, other)
            u = jnp.dot(e.x[...], e.w[1], preferred_element_type=jnp.float32)
        elif q < 3:
            g = jnp.dot(e.x[...], e.w[q * 2], preferred_element_type=jnp.float32)
            u = jnp.dot(e.x[...], e.w[q * 2 + 1], preferred_element_type=jnp.float32)
        else:
            both = jnp.dot(e.x[...], e.w[6], preferred_element_type=jnp.float32)
            g, u = both[:, :128], both[:, 128:]
        scales = jnp.concatenate([e.scl[...]] * (width // 128), axis=1)
        g, u = g * scales, u * scales
        cols = pl.ds(start, width)
        e.units[0, :, cols] = spread(gated(g, u), 0)
        mine = e.units.at[0, :, cols]
        send(mine, e.units.at[1, :, cols], e.zs.at[0], e.zr.at[q], me.peer("z", 1))
        send(mine, e.units.at[3, :, cols], e.zs.at[0], e.zr.at[8 + q], me.peer("z", 3))

    def relay(q):
        slot, step = (1, 1) if q in (0, 3) else (3, 3)
        piece = e.units.at[slot, :, pl.ds(*SPANS[q])]
        drain(e.zr.at[q if slot == 1 else 8 + q], piece)
        send(piece, e.units.at[2, :, pl.ds(*SPANS[q])], e.zs.at[1], e.zr.at[4 + q], me.peer("z", step))

    def unit_wait(slot, q):
        drain(e.zr.at[(slot - 1) * 4 + q], e.units.at[slot, :, pl.ds(*SPANS[q])])

    client_block(0)
    c3.wait()
    scale_row = jnp.concatenate(
        [jnp.sum(jnp.where(eye, e.scl[pl.ds(t, 128), :], 0.0), axis=0, keepdims=True) for t in (0, 128)], axis=1
    )
    mine = e.swap[...] * scale_row
    theirs = e.swin[...] * scale_row
    lead = core == 0
    g = jnp.where(lead, mine, theirs)
    u = jnp.where(lead, theirs, mine)
    high = me.y // 2
    half = pl.ds(pl.multiple_of(core * 128, 128), 128)

    def ref_piece(block, dx, f):
        return e.refs.at[rows(block * FF_HERE + me.plane_piece(dx, f) * PIECE, PIECE), half]

    piece_rows = rows(high * FF_HERE + here * PIECE, PIECE)
    piece_std = spread(gated(g, u), 1)
    e.refs[piece_rows, half] = jnp.where(lead, piece_std[:, :128], piece_std[:, 128:])
    piece = ref_piece(high, 0, 0)
    for n, (dx, f) in enumerate(RING8, 1):
        send(piece, piece, e.xs.at[0], e.xr.at[n], me.plane_peer(dx, f, 0))
    for n, (dx, f) in enumerate([(0, 0)] + RING8):
        send(piece, piece, e.xs.at[1], e.xr.at[8 + n], me.plane_peer(dx, f, 1))
    send(piece, piece, e.csem.at[2], e.crsem.at[5], mate)
    client_block(1)
    client_block(2)
    client_block(3)
    def ref_arrived(k):
        block = high if k == 0 else 1 - high
        for n, (dx, f) in enumerate([(0, 0)] + RING8):
            if k == 1 or n > 0:
                came = ref_piece(block, (4 - dx) % 4, f)
                drain(e.xr.at[8 * k + n], came)
                send(came, came, e.csem.at[2 + k], e.crsem.at[5 + k], mate)

    def mate_done(k):
        part = e.refs.at[pl.ds(0, FF_HERE), half]
        drain(e.crsem.at[5 + k], part)
        drain(e.csem.at[2 + k], part)
        drain(e.xs.at[k], e.refs.at[pl.ds(0, (7 + k) * PIECE), half])

    def align(slot, block, k, first=False):
        left, wide = ((0, 512), (512, 384))[k]
        js = rows(block * FF_HERE, FF_HERE)
        r = e.refs[js, :]
        a = jnp.zeros((FF_HERE, 128), jnp.float32) if first else e.cs[js, :]
        b = jnp.zeros((FF_HERE, 128), jnp.float32) if first else e.ws[js, :]
        for start in range(0, wide, 256):
            width = min(256, wide - start)
            s = jnp.dot(r, e.units[slot, :, pl.ds(left + start, width)], preferred_element_type=jnp.float32)
            v = jnp.exp2(s * EXP_SCALE)
            e.wts[:, pl.ds(start, width)] = v.astype(jnp.bfloat16)
            vs = v * s
            for o in range(0, width, 128):
                a = a + v[:, o : o + 128]
                b = b + vs[:, o : o + 128]
        e.cs[js, :] = a
        e.ws[js, :] = b
        got = lax.dot_general(
            e.wts[:, pl.ds(0, wide)], e.units[slot, :, pl.ds(left, wide)], (((1,), (1,)), ((), ())),
            preferred_element_type=jnp.float32,
        )
        e.num[js, :] = got if first else e.num[js, :] + got

    def to_row(v):
        return jnp.sum(jnp.where(eye, jnp.sum(v, axis=1, keepdims=True), 0.0), axis=0, keepdims=True)

    def join_start(block):
        for q in range(7):
            js = pl.ds(block * FF_HERE + q * 128, 128)
            e.col[block, pl.ds(q, 1), :] = to_row(e.cs[js, :])
            e.col[block, pl.ds(q + 8, 1), :] = to_row(e.ws[js, :])
        return send(e.col.at[block], e.colin.at[block], e.jsem.at[block], e.jsem.at[2 + block], me.peer("y", 2))

    def normalize(block):
        for q in range(7):
            js = pl.ds(block * FF_HERE + q * 128, 128)
            inv = 1.0 / (e.col[block, pl.ds(q, 1), :] + e.colin[block, pl.ds(q, 1), :])
            inv = jnp.sum(jnp.where(eye, inv, 0.0), axis=1, keepdims=True)
            n = (e.num[js, :] * inv).astype(jnp.bfloat16)
            e.nout[0, js, :] = n[:, :128]
            e.nout[1, js, :] = n[:, 128:]
        bs = pl.ds(block * FF_HERE, FF_HERE)
        return send(e.nout.at[other, bs], e.nin.at[bs], e.csem.at[5 + block], e.crsem.at[8 + block], mate)

    def reduce_start(block):
        bs = pl.ds(block * FF_HERE, FF_HERE)
        e.nsum[bs, :] = e.nout[core, bs, :] + e.nin[bs, :]
        hop = (block + high) % 2
        for dx in range(4):
            for f in range(2):
                n = hop * 8 + dx * 2 + f
                src = e.nsum.at[rows(block * FF_HERE + me.plane_piece(dx, f) * PIECE, PIECE)]
                copy = pltpu.make_async_remote_copy(
                    src_ref=src, dst_ref=e.f2.at[n], send_sem=e.xs.at[2], recv_sem=e.xr.at[0],
                    device_id=me.plane_peer(dx, f, hop), device_id_type=MESH,
                )
                if dx == 0 and f == 0:
                    pl.when(hop != 0)(copy.start)
                else:
                    copy.start()

    ref_arrived(0)
    relay(0)
    mate_done(0)
    align(0, high, 0, True)
    align(0, high, 1)
    relay(1)
    unit_wait(1, 1)
    unit_wait(3, 0)
    ref_arrived(1)
    align(1, high, 0)
    align(3, high, 0)
    mate_done(1)
    align(0, 1 - high, 0, True)
    align(0, 1 - high, 1)
    relay(2)
    align(1, 1 - high, 0)
    align(3, 1 - high, 0)
    relay(3)
    unit_wait(1, 2)
    unit_wait(3, 3)
    align(1, 0, 1)
    align(3, 0, 1)
    align(1, 1, 1)
    align(3, 1, 1)
    unit_wait(2, 0)
    unit_wait(2, 1)
    align(2, 0, 0)
    align(2, 1, 0)
    unit_wait(2, 3)
    unit_wait(2, 2)
    align(2, 0, 1)
    c6 = join_start(0)
    align(2, 1, 1)
    c61 = join_start(1)
    c6.wait()
    c7 = [normalize(0)]
    c61.wait()
    c7.append(normalize(1))
    for q in range(7):
        below = e.col[high, pl.ds(q, 1), :] + e.colin[high, pl.ds(q, 1), :]
        above = e.col[high, pl.ds(q + 8, 1), :] + e.colin[high, pl.ds(q + 8, 1), :]
        score_ref[:, pl.ds(q * 128, 128)] = above / below * (1.0 / TOK)
    for block in range(2):
        c7[block].wait()
        reduce_start(block)
    drain(e.xr.at[0], e.f2.at[pl.ds(1, 15)])
    drain(e.xs.at[2], e.f2.at[pl.ds(1, 15)])
    total = e.nsum[piece_rows, :].astype(jnp.float32)
    for n in range(1, 16):
        total = total + e.f2[n].astype(jnp.float32)
    mine = e.fin.at[core, here]
    mine[...] = total.astype(jnp.bfloat16)
    send(mine, mine, e.csem.at[7], e.crsem.at[10], mate)
    for n, (dx, f) in enumerate(RING8):
        send(mine, mine, e.xs.at[3], e.xr.at[16 + n], me.plane_peer(dx, f, 0))
    for n, (dx, f) in enumerate(RING8):
        came = e.fin.at[core, me.plane_piece(4 - dx, f)]
        drain(e.xr.at[16 + n], came)
        send(came, came, e.csem.at[7], e.crsem.at[10], mate)
    drain(e.xs.at[3], e.fin.at[0, pl.ds(1, 7)])
    for _ in range(2):
        drain(e.zs.at[0], e.units.at[0])
    drain(e.zs.at[1], e.units.at[2])
    drain(e.crsem.at[10], e.fin.at[0])
    drain(e.csem.at[7], e.fin.at[0])
    fin_ref[...] = e.fin[...]


def finish_kernel(fin_ref, mean_ref, merged_ref, score_ref):
    for s in range(8):
        for h in range(2):
            merged_ref[pl.ds(s * PIECE, PIECE), pl.ds(h * 128, 128)] = fin_ref[h, s].astype(jnp.float32) * (1.0 / 16)
    score_ref[...] = mean_ref[...]


def layout():
    bf, f32 = jnp.bfloat16, jnp.float32
    dma = pltpu.SemaphoreType.DMA
    vm = pltpu.VMEM
    widths = [w for _, w in PARTS]
    return {
        "tabs": vm((8, 512, 512), bf),
        "accs": vm((TOK, HALF), bf),
        "outs": vm((TOK, HALF), bf),
        "cins": vm((TOK, HALF), bf),
        "r1s": [vm((3, 64, w), bf) for w in widths],
        "a1s": [vm((64, w), bf) for w in widths],
        "r2s": [vm((3, 16, w), bf) for w in widths],
        "a2s": [vm((16, w), bf) for w in widths],
        "r3s": [vm((3, 16, w), bf) for w in widths],
        "fulls": [vm((2, TOK, w), bf) for w in widths],
        "pick": vm((TOK, 512), bf),
        "x": vm((TOK, D), bf),
        "w": vm((7, D, 256), bf),
        "rw": vm((2, 256, FF_HERE), bf),
        "rt": vm((2, FF_HERE, 256), bf),
        "wr": vm((PIECE, D), bf),
        "acc": vm((1, TOK, 256), f32),
        "scl": vm((TOK, 128), f32),
        "swap": vm((PIECE, TOK), f32),
        "swin": vm((PIECE, TOK), f32),
        "refs": vm((JOINT, TOK), bf),
        "units": vm((4, TOK, FF_HERE), bf),
        "wts": vm((FF_HERE, 512), bf),
        "num": vm((JOINT, TOK), f32),
        "cs": vm((JOINT, 128), f32),
        "ws": vm((JOINT, 128), f32),
        "col": vm((2, 16, 128), f32),
        "colin": vm((2, 16, 128), f32),
        "nout": vm((2, JOINT, 128), bf),
        "nin": vm((JOINT, 128), bf),
        "nsum": vm((JOINT, 128), bf),
        "f2": vm((16, PIECE, 128), bf),
        "fin": vm((2, 8, PIECE, 128), bf),
        "tsem": dma((8,)),
        "ssem": dma((NP,)),
        "rsem": dma((NP, 6)),
        "wsem": dma((8,)),
        "rwsem": dma((1,)),
        "wshare": dma((2,)),
        "csem": dma((8,)),
        "crsem": dma((11,)),
        "jsem": dma((4,)),
        "zs": dma((2,)),
        "zr": dma((12,)),
        "xs": dma((4,)),
        "xr": dma((23,)),
    }


class Refs:
    def __init__(self, scratch):
        left = list(scratch)
        for name, shape in layout().items():
            if isinstance(shape, list):
                setattr(self, name, [left.pop(0) for _ in shape])
            else:
                setattr(self, name, left.pop(0))


def body(token_ids, embed_table, norm_gain, client_gate, client_up, ref_gate, ref_up):
    shapes = []
    for shape in layout().values():
        shapes += shape if isinstance(shape, list) else [shape]
    vmem = pl.BlockSpec(memory_space=pltpu.VMEM)
    hbm = pl.BlockSpec(memory_space=pl.ANY)
    f32 = jnp.float32
    fin, mean = pl.pallas_call(
        kernel,
        out_shape=(
            jax.ShapeDtypeStruct((2, 8, PIECE, 128), jnp.bfloat16),
            jax.ShapeDtypeStruct((1, FF_HERE), f32),
        ),
        in_specs=[vmem, vmem, hbm, hbm, hbm, hbm, hbm],
        out_specs=(vmem, vmem),
        scratch_shapes=shapes,
        compiler_params=pltpu.CompilerParams(collective_id=0, has_side_effects=True, vmem_limit_bytes=60 << 20),
        name="soft_alignment",
    )(token_ids[None, :], norm_gain[None, :], embed_table, client_gate, client_up, ref_gate, ref_up)
    return pl.pallas_call(
        finish_kernel,
        out_shape=(jax.ShapeDtypeStruct((FF_HERE, TOK), f32), jax.ShapeDtypeStruct((1, FF_HERE), f32)),
        in_specs=[vmem, vmem],
        out_specs=(vmem, vmem),
        name="finish",
    )(fin, mean)


def solution(mesh):
    in_specs = (
        P(),
        P(("client", "unit"), None),
        P(),
        P("client", None, "unit"),
        P("client", None, "unit"),
        P("client", "unit"),
        P("client", "unit"),
    )
    out_specs = (P("unit", None), P("client", "unit"))
    return jax.shard_map(body, mesh=mesh, in_specs=in_specs, out_specs=out_specs, check_vma=False)
```

```python
import jax
import jax.numpy as jnp
from jax import lax
from jax.experimental import pallas as pl
from jax.experimental.pallas import tpu as pltpu
from jax.sharding import PartitionSpec as P

sharpness = 40.0
MESH = pl.DeviceIdType.MESH

TOK = 256
D = 4096
HALF = D // 2
PARTS = ((0, 384), (384, 384), (768, 384), (1152, 256), (1408, 256), (1664, 384))
ORDERS = ("xyz", "yzx", "zxy") * 2
NP = len(PARTS)


class Place:
    def __init__(self):
        client = lax.axis_index("client")
        unit = lax.axis_index("unit")
        self.core = client % 2
        self.x = (client // 2) % 4
        self.y = (unit % 2) * 2 + client // 8
        self.z = unit // 2

    def at(self, axis):
        return getattr(self, axis)

    def peer(self, axis, step):
        x, y, z, core = self.x, self.y, self.z, self.core
        if axis == "x":
            x = (x + step) % 4
        elif axis == "y":
            y = (y + step) % 4
        elif axis == "z":
            z = (z + step) % 4
        else:
            core = 1 - core
        return {"client": (y % 2) * 8 + x * 2 + core, "unit": z * 2 + y // 2}


    def plane_peer(self, dx, flip, hflip, cflip=0):
        x = (self.x + dx) % 4
        low = (self.y % 2 + flip) % 2
        high = (self.y // 2 + hflip) % 2
        return {"client": low * 8 + x * 2 + (self.core + cflip) % 2, "unit": self.z * 2 + high}

    def plane_piece(self, dx, flip):
        return ((self.x + dx) % 4) * 2 + (self.y % 2 + flip) % 2


def send(src, dst, ssem, rsem, peer):
    copy = pltpu.make_async_remote_copy(
        src_ref=src, dst_ref=dst, send_sem=ssem, recv_sem=rsem, device_id=peer, device_id_type=MESH
    )
    copy.start()
    return copy


def drain(sem, ref):
    pltpu.make_async_copy(ref, ref, sem).wait()


def rows(start, size):
    return pl.ds(pl.multiple_of(start, size), size)

FF_HERE = 896
PIECE = 112
JOINT = 2 * FF_HERE
SHARES = (4, 3, 3, 3, 2, 0)
SPANS = ((0, 256), (256, 256), (512, 256), (768, 128))
RING8 = [(dx, f) for dx in range(4) for f in range(2)][1:]
STEPS = 2
CROSS = [(dx, f, c) for dx in range(4) for f in range(2) for c in range(2)][1:]
RING16 = [(dx, f, h) for h in range(2) for dx in range(4) for f in range(2)][1:]
EXP_SCALE = sharpness / TOK * 1.4426950408889634


def spread(h, axis):
    center = jnp.mean(h, axis=axis, keepdims=True)
    shifted = h - center
    width = jnp.sqrt(jnp.mean(shifted * shifted, axis=axis, keepdims=True) + 1e-06)
    return (shifted / width).astype(jnp.bfloat16)


def gated(g, u):
    return g / (1.0 + jnp.exp(-g)) * u


def kernel(ids_hbm, gain_hbm, table_ref, cg_ref, cu_ref, rg_ref, ru_ref, fin_ref, score_ref, *scratch):
    e = Refs(scratch)
    me = Place()
    core, other = me.core, 1 - me.core
    mate = me.peer("core", 1)
    client = lax.axis_index("client")
    ssem, rsem = e.ssem, e.rsem

    ids_ref, gain_ref = e.ids, e.gain
    small = [
        pltpu.make_async_copy(ids_hbm, ids_ref, e.rwsem.at[1]),
        pltpu.make_async_copy(gain_hbm, gain_ref, e.rwsem.at[2]),
    ]
    small[0].start()
    def table_load(k):
        half = other if k < 4 else core
        at = pl.multiple_of(half * HALF + k % 4 * 512, 512)
        load = pltpu.make_async_copy(table_ref.at[:, pl.ds(at, 512)], e.tabs.at[k], e.tsem.at[k])
        load.start()
        return load

    loads = [table_load(k) for k in range(4)]
    for t, src in enumerate((rg_ref, ru_ref)):
        pltpu.make_async_copy(src, e.rw.at[t], e.rwsem.at[0]).start()
    loads += [table_load(k) for k in range(4, 8)]
    small[1].start()

    barrier = pltpu.get_barrier_semaphore()
    peers = [me.plane_peer(*r) for r in RING16] + [me.peer("z", d) for d in (1, 2, 3)] + [mate]
    peers += [me.plane_peer(dx, f, 0, 1) for dx, f in RING8]
    for peer in peers:
        pl.semaphore_signal(barrier, inc=1, device_id=peer, device_id_type=MESH)

    eye = lax.broadcasted_iota(jnp.int32, (128, 128), 0) == lax.broadcasted_iota(jnp.int32, (128, 128), 1)
    start = (client * 8 + lax.axis_index("unit")) * 512
    table_rows = (start + lax.broadcasted_iota(jnp.int32, (1, 512), 1)).astype(jnp.float32)
    small[0].wait()
    for t in range(2):
        wide = ids_ref[:, pl.ds(t * 128, 128)].astype(jnp.float32)
        tall = jnp.sum(jnp.where(eye, wide, 0.0), axis=1, keepdims=True)
        e.pick[pl.ds(t * 128, 128), :] = jnp.where(tall == table_rows, 1.0, 0.0).astype(jnp.bfloat16)

    def looked_up(k):
        loads[k].wait()
        return jnp.dot(e.pick[...], e.tabs[k], preferred_element_type=jnp.float32).astype(jnp.bfloat16)

    chunks = [pl.ds(k * 512, 512) for k in range(4)]
    for k in range(4):
        e.outs[:, chunks[k]] = looked_up(k)
    here = me.plane_piece(0, 0)
    depth = pl.ds(pl.multiple_of(client * 256, 256), 256)
    drain(e.rwsem.at[0], e.rw)
    for t in range(2):
        e.rt[t] = e.rw[t].T
    e.wr[:, depth] = e.rt[core, rows(here * PIECE, PIECE), :]
    shared = []

    def share(count):
        for _ in range(count):
            n = len(shared)
            dx, f, c = CROSS[n]
            src = e.rt.at[(core + c) % 2, rows(me.plane_piece(dx, f) * PIECE, PIECE)]
            shared.append(send(src, e.wr.at[:, depth], e.wshare.at[0], e.wshare.at[1], me.plane_peer(dx, f, 0, c)))

    pl.semaphore_wait(barrier, len(peers))
    sent = []
    for k in range(4):
        sent.append(send(e.outs.at[:, chunks[k]], e.cins.at[:, chunks[k]], e.csem.at[0], e.crsem.at[k], mate))
    share(SHARES[0])
    for k in range(4):
        e.accs[:, chunks[k]] = looked_up(4 + k)
    wload = {}
    for q in range(3):
        for k, src in enumerate((cg_ref, cu_ref)):
            load = pltpu.make_async_copy(
                src.at[0, :, pl.ds(q * 256, 256)], e.w.at[q * 2 + k], e.wsem.at[q * 2 + k]
            )
            load.start()
            wload[q, k] = load
    for k, src in enumerate((cg_ref, cu_ref)):
        load = pltpu.make_async_copy(
            src.at[0, :, pl.ds(768, 128)], e.w.at[6, :, pl.ds(k * 128, 128)], e.wsem.at[6 + k]
        )
        load.start()
        wload[3, k] = load

    small[1].wait()
    for k in range(4):
        sent[k].wait_recv()
        e.accs[:, chunks[k]] = e.accs[:, chunks[k]] + e.cins[:, chunks[k]]
    for p in range(NP):
        axis = ORDERS[p][0]
        for d in (1, 2, 3):
            to = (me.at(axis) + d) % 4
            src = e.accs.at[rows(to * 64, 64), pl.ds(*PARTS[p])]
            send(src, e.r1s[p].at[d - 1], ssem.at[p], rsem.at[p, 0], me.peer(axis, d))

    share(SHARES[1])
    for p in range(NP):
        drain(rsem.at[p, 0], e.r1s[p])
        drain(ssem.at[p], e.r1s[p])
        own = e.accs[rows(me.at(ORDERS[p][0]) * 64, 64), pl.ds(*PARTS[p])]
        e.a1s[p][...] = (own + e.r1s[p][0]) + (e.r1s[p][1] + e.r1s[p][2])
        axis = ORDERS[p][1]
        for d in (1, 2, 3):
            to = (me.at(axis) + d) % 4
            send(e.a1s[p].at[rows(to * 16, 16)], e.r2s[p].at[d - 1], ssem.at[p], rsem.at[p, 1], me.peer(axis, d))
    drain(e.csem.at[0], e.outs)
    share(SHARES[2])
    for p in range(NP):
        drain(rsem.at[p, 1], e.r2s[p])
        drain(ssem.at[p], e.r2s[p])
        own = e.a1s[p][rows(me.at(ORDERS[p][1]) * 16, 16), :]
        e.a2s[p][...] = (own + e.r2s[p][0]) + (e.r2s[p][1] + e.r2s[p][2])
        axis = ORDERS[p][2]
        for d in (1, 2, 3):
            send(e.a2s[p], e.r3s[p].at[d - 1], ssem.at[p], rsem.at[p, 2], me.peer(axis, d))
    share(SHARES[3])
    for p in range(NP):
        drain(rsem.at[p, 2], e.r3s[p])
        drain(ssem.at[p], e.r3s[p])
        base = me.at(ORDERS[p][0]) * 64 + me.at(ORDERS[p][1]) * 16
        piece = e.fulls[p].at[core, rows(base, 16)]
        piece[...] = (e.a2s[p][...] + e.r3s[p][0]) + (e.r3s[p][1] + e.r3s[p][2])
        axis = ORDERS[p][1]
        for d in (1, 2, 3):
            send(piece, piece, ssem.at[p], rsem.at[p, 3], me.peer(axis, d))
    share(SHARES[4])
    for p in range(NP):
        drain(rsem.at[p, 3], e.r2s[p])
        drain(ssem.at[p], e.r2s[p])
        axis = ORDERS[p][0]
        piece = e.fulls[p].at[core, rows(me.at(axis) * 64, 64)]
        for d in (1, 2, 3):
            send(piece, piece, ssem.at[p], rsem.at[p, 4], me.peer(axis, d))
    share(SHARES[5])
    def prepare(p, h, first=False):
        off, width = PARTS[p]
        cols = pl.ds(pl.multiple_of(h * HALF + off, 128), width)
        v = e.fulls[p][h].astype(jnp.float32)
        squares = v * v
        total = squares[:, :128]
        for o in range(128, width, 128):
            total = total + squares[:, o : o + 128]
        e.scl[...] = total if first else e.scl[...] + total
        e.x[:, cols] = (v * gain_ref[:, cols]).astype(jnp.bfloat16)

    s6 = []
    for p in range(NP):
        drain(rsem.at[p, 4], e.r1s[p])
        drain(ssem.at[p], e.r1s[p])
        piece = e.fulls[p].at[core]
        s6.append(send(piece, piece, ssem.at[p], rsem.at[p, 5], mate))
        prepare(p, core, p == 0)
    apart = e.wr.at[:, pl.ds(256, D - 256)]
    drain(e.wshare.at[1], apart)
    drain(e.wshare.at[0], apart)

    def half_of(h):
        return pl.ds(pl.multiple_of(h * HALF, HALF), HALF)

    def ref_half(h):
        return lax.dot_general(
            e.wr[:, half_of(h)], e.x[:, half_of(h)], (((1,), (1,)), ((), ())), preferred_element_type=jnp.float32
        )

    def client_half(k, h):
        return jnp.dot(e.x[:, half_of(h)], e.w[k, half_of(h), :], preferred_element_type=jnp.float32)

    e.swap[...] = ref_half(core)
    for k in range(2):
        wload[0, k].wait()
    e.acc[0] = client_half(0, core)
    for p in range(NP):
        s6[p].wait()
        prepare(p, other)
    e.swap[...] = e.swap[...] + ref_half(other)
    c3 = send(e.swap, e.swin, e.csem.at[1], e.crsem.at[4], mate)
    scale = lax.rsqrt(jnp.sum(e.scl[...], axis=1, keepdims=True) * (1.0 / D) + 1e-05)
    e.scl[...] = jnp.broadcast_to(scale, (TOK, 128))

    def client_block(q):
        start, width = SPANS[q]
        for k in range(2):
            if q > 0:
                wload[q, k].wait()
        if q == 0:
            g = e.acc[0] + client_half(0, other)
            u = jnp.dot(e.x[...], e.w[1], preferred_element_type=jnp.float32)
        elif q < 3:
            g = jnp.dot(e.x[...], e.w[q * 2], preferred_element_type=jnp.float32)
            u = jnp.dot(e.x[...], e.w[q * 2 + 1], preferred_element_type=jnp.float32)
        else:
            both = jnp.dot(e.x[...], e.w[6], preferred_element_type=jnp.float32)
            g, u = both[:, :128], both[:, 128:]
        scales = jnp.concatenate([e.scl[...]] * (width // 128), axis=1)
        g, u = g * scales, u * scales
        cols = pl.ds(start, width)
        e.units[0, :, cols] = spread(gated(g, u), 0)
        mine = e.units.at[0, :, cols]
        send(mine, e.units.at[1, :, cols], e.zs.at[0], e.zr.at[q], me.peer("z", 1))
        send(mine, e.units.at[3, :, cols], e.zs.at[0], e.zr.at[8 + q], me.peer("z", 3))

    def relay(q):
        slot, step = (1, 1) if q in (0, 3) else (3, 3)
        piece = e.units.at[slot, :, pl.ds(*SPANS[q])]
        drain(e.zr.at[q if slot == 1 else 8 + q], piece)
        send(piece, e.units.at[2, :, pl.ds(*SPANS[q])], e.zs.at[1], e.zr.at[4 + q], me.peer("z", step))

    def unit_wait(slot, q):
        drain(e.zr.at[(slot - 1) * 4 + q], e.units.at[slot, :, pl.ds(*SPANS[q])])

    client_block(0)
    c3.wait()
    scale_row = jnp.concatenate(
        [jnp.sum(jnp.where(eye, e.scl[pl.ds(t, 128), :], 0.0), axis=0, keepdims=True) for t in (0, 128)], axis=1
    )
    mine = e.swap[...] * scale_row
    theirs = e.swin[...] * scale_row
    lead = core == 0
    g = jnp.where(lead, mine, theirs)
    u = jnp.where(lead, theirs, mine)
    high = me.y // 2
    half = pl.ds(pl.multiple_of(core * 128, 128), 128)

    def ref_piece(block, dx, f):
        return e.refs.at[rows(block * FF_HERE + me.plane_piece(dx, f) * PIECE, PIECE), half]

    piece_rows = rows(high * FF_HERE + here * PIECE, PIECE)
    piece_std = spread(gated(g, u), 1)
    e.refs[piece_rows, half] = jnp.where(lead, piece_std[:, :128], piece_std[:, 128:])
    piece = ref_piece(high, 0, 0)
    for dx, f in RING8:
        send(piece, piece, e.xs.at[0], e.xr.at[0], me.plane_peer(dx, f, 0))
    for dx, f in [(0, 0)] + RING8:
        send(piece, piece, e.xs.at[1], e.xr.at[1], me.plane_peer(dx, f, 1))
    client_block(1)
    client_block(2)
    client_block(3)
    def ref_arrived(k):
        block = high if k == 0 else 1 - high
        drain(e.xr.at[k], e.refs.at[pl.ds(0, (7 + k) * PIECE), half])
        part = e.refs.at[rows(block * FF_HERE, FF_HERE), half]
        send(part, part, e.csem.at[2 + k], e.crsem.at[5 + k], mate)

    def mate_done(k):
        part = e.refs.at[pl.ds(0, FF_HERE), half]
        drain(e.crsem.at[5 + k], part)
        drain(e.csem.at[2 + k], part)
        drain(e.xs.at[k], e.refs.at[pl.ds(0, (7 + k) * PIECE), half])

    def align(slot, block, k, first=False):
        left, wide = ((0, 512), (512, 384))[k]
        js = rows(block * FF_HERE, FF_HERE)
        r = e.refs[js, :]
        a = jnp.zeros((FF_HERE, 128), jnp.float32) if first else e.cs[js, :]
        b = jnp.zeros((FF_HERE, 128), jnp.float32) if first else e.ws[js, :]
        for start in range(0, wide, 256):
            width = min(256, wide - start)
            s = jnp.dot(r, e.units[slot, :, pl.ds(left + start, width)], preferred_element_type=jnp.float32)
            v = jnp.exp2(s * EXP_SCALE)
            e.wts[:, pl.ds(start, width)] = v.astype(jnp.bfloat16)
            vs = v * s
            for o in range(0, width, 128):
                a = a + v[:, o : o + 128]
                b = b + vs[:, o : o + 128]
        e.cs[js, :] = a
        e.ws[js, :] = b
        got = lax.dot_general(
            e.wts[:, pl.ds(0, wide)], e.units[slot, :, pl.ds(left, wide)], (((1,), (1,)), ((), ())),
            preferred_element_type=jnp.float32,
        )
        e.num[js, :] = got if first else e.num[js, :] + got

    def to_row(v):
        return jnp.sum(jnp.where(eye, jnp.sum(v, axis=1, keepdims=True), 0.0), axis=0, keepdims=True)

    def join_start(block):
        for q in range(7):
            js = pl.ds(block * FF_HERE + q * 128, 128)
            e.col[block, pl.ds(q, 1), :] = to_row(e.cs[js, :])
            e.col[block, pl.ds(q + 8, 1), :] = to_row(e.ws[js, :])
        return send(e.col.at[block], e.colin.at[block], e.jsem.at[block], e.jsem.at[2 + block], me.peer("y", 2))

    def normalize(block):
        for q in range(7):
            js = pl.ds(block * FF_HERE + q * 128, 128)
            inv = 1.0 / (e.col[block, pl.ds(q, 1), :] + e.colin[block, pl.ds(q, 1), :])
            inv = jnp.sum(jnp.where(eye, inv, 0.0), axis=1, keepdims=True)
            n = (e.num[js, :] * inv).astype(jnp.bfloat16)
            e.nout[0, js, :] = n[:, :128]
            e.nout[1, js, :] = n[:, 128:]
        bs = pl.ds(block * FF_HERE, FF_HERE)
        return send(e.nout.at[other, bs], e.nin.at[bs], e.csem.at[5 + block], e.crsem.at[8 + block], mate)

    def reduce_start(block):
        bs = pl.ds(block * FF_HERE, FF_HERE)
        e.nsum[bs, :] = e.nout[core, bs, :] + e.nin[bs, :]
        hop = (block + high) % 2
        for dx in range(4):
            for f in range(2):
                n = hop * 8 + dx * 2 + f
                src = e.nsum.at[rows(block * FF_HERE + me.plane_piece(dx, f) * PIECE, PIECE)]
                copy = pltpu.make_async_remote_copy(
                    src_ref=src, dst_ref=e.f2.at[n], send_sem=e.xs.at[2], recv_sem=e.xr.at[2],
                    device_id=me.plane_peer(dx, f, hop), device_id_type=MESH,
                )
                if dx == 0 and f == 0:
                    pl.when(hop != 0)(copy.start)
                else:
                    copy.start()

    ref_arrived(0)
    relay(0)
    mate_done(0)
    align(0, high, 0, True)
    align(0, high, 1)
    relay(1)
    unit_wait(1, 1)
    unit_wait(3, 0)
    ref_arrived(1)
    align(1, high, 0)
    align(3, high, 0)
    mate_done(1)
    align(0, 1 - high, 0, True)
    align(0, 1 - high, 1)
    relay(2)
    align(1, 1 - high, 0)
    align(3, 1 - high, 0)
    relay(3)
    unit_wait(1, 2)
    unit_wait(3, 3)
    align(1, 0, 1)
    align(3, 0, 1)
    align(1, 1, 1)
    align(3, 1, 1)
    unit_wait(2, 0)
    unit_wait(2, 1)
    align(2, 0, 0)
    align(2, 1, 0)
    unit_wait(2, 3)
    unit_wait(2, 2)
    align(2, 0, 1)
    c6 = join_start(0)
    align(2, 1, 1)
    c61 = join_start(1)
    c6.wait()
    c7 = [normalize(0)]
    c61.wait()
    c7.append(normalize(1))
    for q in range(7):
        below = e.col[high, pl.ds(q, 1), :] + e.colin[high, pl.ds(q, 1), :]
        above = e.col[high, pl.ds(q + 8, 1), :] + e.colin[high, pl.ds(q + 8, 1), :]
        score_ref[:, pl.ds(q * 128, 128)] = above / below * (1.0 / TOK)
    for block in range(2):
        c7[block].wait()
        reduce_start(block)
    drain(e.xr.at[2], e.f2.at[pl.ds(1, 15)])
    drain(e.xs.at[2], e.f2.at[pl.ds(1, 15)])
    total = e.nsum[piece_rows, :].astype(jnp.float32)
    for n in range(1, 16):
        total = total + e.f2[n].astype(jnp.float32)
    mine = e.fin.at[core, here]
    mine[...] = total.astype(jnp.bfloat16)
    for dx, f in RING8:
        send(mine, mine, e.xs.at[3], e.xr.at[3], me.plane_peer(dx, f, 0))
    drain(e.xr.at[3], e.fin.at[0, pl.ds(1, 7)])
    send(e.fin.at[core], e.fin.at[core], e.csem.at[7], e.crsem.at[10], mate)
    drain(e.xs.at[3], e.fin.at[0, pl.ds(1, 7)])
    for _ in range(2):
        drain(e.zs.at[0], e.units.at[0])
    drain(e.zs.at[1], e.units.at[2])
    drain(e.crsem.at[10], e.fin.at[0])
    drain(e.csem.at[7], e.fin.at[0])
    fin_ref[...] = e.fin[...]


def finish_kernel(fin_ref, mean_ref, merged_ref, score_ref):
    for s in range(8 // STEPS):
        for h in range(2):
            merged_ref[pl.ds(s * PIECE, PIECE), pl.ds(h * 128, 128)] = fin_ref[h, s].astype(jnp.float32) * (1.0 / 16)
    score_ref[...] = mean_ref[...]


def layout():
    bf, f32 = jnp.bfloat16, jnp.float32
    dma = pltpu.SemaphoreType.DMA
    vm = pltpu.VMEM
    widths = [w for _, w in PARTS]
    return {
        "tabs": vm((8, 512, 512), bf),
        "accs": vm((TOK, HALF), bf),
        "outs": vm((TOK, HALF), bf),
        "cins": vm((TOK, HALF), bf),
        "r1s": [vm((3, 64, w), bf) for w in widths],
        "a1s": [vm((64, w), bf) for w in widths],
        "r2s": [vm((3, 16, w), bf) for w in widths],
        "a2s": [vm((16, w), bf) for w in widths],
        "r3s": [vm((3, 16, w), bf) for w in widths],
        "fulls": [vm((2, TOK, w), bf) for w in widths],
        "ids": vm((1, TOK), jnp.int32),
        "gain": vm((1, D), f32),
        "pick": vm((TOK, 512), bf),
        "x": vm((TOK, D), bf),
        "w": vm((7, D, 256), bf),
        "rw": vm((2, 256, FF_HERE), bf),
        "rt": vm((2, FF_HERE, 256), bf),
        "wr": vm((PIECE, D), bf),
        "acc": vm((1, TOK, 256), f32),
        "scl": vm((TOK, 128), f32),
        "swap": vm((PIECE, TOK), f32),
        "swin": vm((PIECE, TOK), f32),
        "refs": vm((JOINT, TOK), bf),
        "units": vm((4, TOK, FF_HERE), bf),
        "wts": vm((FF_HERE, 512), bf),
        "num": vm((JOINT, TOK), f32),
        "cs": vm((JOINT, 128), f32),
        "ws": vm((JOINT, 128), f32),
        "col": vm((2, 16, 128), f32),
        "colin": vm((2, 16, 128), f32),
        "nout": vm((2, JOINT, 128), bf),
        "nin": vm((JOINT, 128), bf),
        "nsum": vm((JOINT, 128), bf),
        "f2": vm((16, PIECE, 128), bf),
        "fin": vm((2, 8, PIECE, 128), bf),
        "tsem": dma((8,)),
        "ssem": dma((NP,)),
        "rsem": dma((NP, 6)),
        "wsem": dma((8,)),
        "rwsem": dma((3,)),
        "wshare": dma((2,)),
        "csem": dma((8,)),
        "crsem": dma((11,)),
        "jsem": dma((4,)),
        "zs": dma((2,)),
        "zr": dma((12,)),
        "xs": dma((4,)),
        "xr": dma((4,)),
    }


class Refs:
    def __init__(self, scratch):
        left = list(scratch)
        for name, shape in layout().items():
            if isinstance(shape, list):
                setattr(self, name, [left.pop(0) for _ in shape])
            else:
                setattr(self, name, left.pop(0))


def body(token_ids, embed_table, norm_gain, client_gate, client_up, ref_gate, ref_up):
    shapes = []
    for shape in layout().values():
        shapes += shape if isinstance(shape, list) else [shape]
    vmem = pl.BlockSpec(memory_space=pltpu.VMEM)
    hbm = pl.BlockSpec(memory_space=pl.ANY)
    f32 = jnp.float32
    fin, mean = pl.pallas_call(
        kernel,
        out_shape=(
            jax.ShapeDtypeStruct((2, 8, PIECE, 128), jnp.bfloat16),
            jax.ShapeDtypeStruct((1, FF_HERE), f32),
        ),
        in_specs=[hbm] * 7,
        out_specs=(vmem, vmem),
        scratch_shapes=shapes,
        compiler_params=pltpu.CompilerParams(collective_id=0, has_side_effects=True, vmem_limit_bytes=60 << 20),
        name="soft_alignment",
    )(token_ids[None, :], norm_gain[None, :], embed_table, client_gate, client_up, ref_gate, ref_up)
    return pl.pallas_call(
        finish_kernel,
        out_shape=(jax.ShapeDtypeStruct((FF_HERE, TOK), f32), jax.ShapeDtypeStruct((1, FF_HERE), f32)),
        grid=(STEPS,),
        in_specs=[
            pl.BlockSpec((2, 8 // STEPS, PIECE, 128), lambda t: (0, t, 0, 0)),
            pl.BlockSpec((1, FF_HERE), lambda t: (0, 0)),
        ],
        out_specs=(
            pl.BlockSpec((FF_HERE // STEPS, TOK), lambda t: (t, 0)),
            pl.BlockSpec((1, FF_HERE), lambda t: (0, 0)),
        ),
        name="finish",
    )(fin, mean)


def solution(mesh):
    in_specs = (
        P(),
        P(("client", "unit"), None),
        P(),
        P("client", None, "unit"),
        P("client", None, "unit"),
        P("client", "unit"),
        P("client", "unit"),
    )
    out_specs = (P("unit", None), P("client", "unit"))
    return jax.shard_map(body, mesh=mesh, in_specs=in_specs, out_specs=out_specs, check_vma=False)
```
